256 devices in a mesh: chan: 32 (over y, x, core), tile: 8 (over z).
Axes of the slice: x: 4, y: 4, z: 8, core: 2. Of those that a mesh axis runs over, the one named last changes fastest.
Arguments:
- generator: bfloat16 [128, 1024, 1024], P('chan', 'tile'), as said below
- hamiltonian: bfloat16 [128, 1024, 1024], P('chan', 'tile')
- chan_sizes: int32 [128], P('chan'), may hold values from 512 to 1024
- pair_occupation: int32 [2, 128, 1024], P(None, 'chan'), may hold values 0 or 1
- recoupled_occupation: int32 [2, 512, 512], P(None, ('chan', 'tile')), may hold values 0 or 1
- recouple_map: int32 [512, 512], P(('chan', 'tile')), may hold values from 0 to 511, each once within a row
- recouple_weights: float32 [512, 512, 512], P(('chan', 'tile')), may hold values from -2 to 2
Outputs:
- commutator: bfloat16 [128, 1024, 1024], P('chan', 'tile')
The draws below stay inside these ranges and needn't reach their ends.
Inputs may be any that keep to these rules, and one draw needn't show every extreme that they name: generator[c] is antisymmetric and hamiltonian[c] is symmetric in every channel.
All inputs are finite; a program needn't handle non-finite values. No bound on the sum of `pair_occupation` or of `recoupled_occupation` on one device may be relied on, other than what follows from the above.
Results may differ from the reference program's by a relative error of at most 0.0045.
Values may be sent and summed in bfloat16 or wider, within the bound.
A program may use at most 128 MiB of HBM per device.

```python
import math
import jax
import jax.numpy as jnp
from jax import lax

M = 1024
CH_DEV = 4
NCH = 128
MP = 512
PH_DEV = 2
NPH = 512
N_CHAN = 32
N_TILE = 8


def pair_block(key, symmetric):
    base = jax.random.normal(key, (NCH, M, M), jnp.float32) * M ** (-0.25) / math.sqrt(2.0)
    flipped = jnp.swapaxes(base, 1, 2)
    if symmetric:
        return (base + flipped).astype(jnp.bfloat16)
    return (base - flipped).astype(jnp.bfloat16)


def draw_generator(key, part):
    return pair_block(jax.random.fold_in(key, 11), False)


def draw_hamiltonian(key, part):
    return pair_block(jax.random.fold_in(key, 12), True)


def place_ends(array, own_key, least, high):
    extent = array.shape
    spot = [jax.random.randint(jax.random.fold_in(own_key, axis), (), 0, extent[axis]) for axis in range(len(extent))]
    array = array.at[tuple(spot)].set(least)
    longest = extent.index(max(extent))
    spot[longest] = (spot[longest] + 1) % extent[longest]
    return array.at[tuple(spot)].set(high)


def block_scale(own_key, shape, pieces, low, high):
    def one(position, shards_of):
        draws = jax.random.uniform(jax.random.fold_in(jax.random.fold_in(own_key, 6), position), (shards_of,), jnp.float32, low / len(pieces), high / len(pieces))
        return jnp.repeat(jnp.exp(draws), shape[position] // shards_of).reshape((-1,) + (1,) * (len(shape) - position - 1))

    level = one(*pieces[0])
    for cut in pieces[1:]:
        level = level * one(*cut)
    return level


def setup_inputs(seed: int = 0) -> dict:
    splits = jax.random.split(jax.random.key(seed), 8)
    return {
        "generator": draw_generator(jax.random.fold_in(splits[7], 71), 0),
        "hamiltonian": draw_hamiltonian(jax.random.fold_in(splits[7], 71), 0),
        "chan_sizes": place_ends(jax.random.randint(splits[2], (NCH,), M // 2, M + 1), jax.random.fold_in(splits[2], 1), M // 2, M).astype(jnp.int32),
        "pair_occupation": place_ends((jax.random.randint(splits[3], (2, NCH, M), 0, 4) < 1).astype(jnp.int32), jax.random.fold_in(splits[3], 1), 0, 1),
        "recoupled_occupation": place_ends((jax.random.randint(splits[4], (2, NPH, MP), 0, 2) < 1).astype(jnp.int32), jax.random.fold_in(splits[4], 1), 0, 1),
        "recouple_map": jax.vmap(lambda own: jax.random.permutation(own, MP))(jax.random.split(splits[5], NPH)).reshape((NPH, MP)).astype(jnp.int32),
        "recouple_weights": jnp.clip(jax.random.uniform(splits[6], (NPH, MP, MP), jnp.float32, -2.0, 2.0) * block_scale(splits[6], (NPH, MP, MP), ((0, 256),), -0.4, 0.0), -2.0, 2.0),
    }


def to_recoupled(values):
    tile_rows = M // N_TILE
    group_rows = CH_DEV * tile_rows // N_CHAN
    shaped = values.reshape(N_CHAN, CH_DEV, N_TILE, tile_rows, M)
    shaped = jnp.transpose(shaped, (0, 2, 1, 3, 4))
    shaped = shaped.reshape(N_CHAN, N_TILE, N_CHAN, group_rows, PH_DEV, MP)
    shaped = jnp.transpose(shaped, (2, 1, 4, 0, 3, 5))
    return shaped.reshape(NPH, MP, MP)


def from_recoupled(values):
    tile_rows = M // N_TILE
    group_rows = CH_DEV * tile_rows // N_CHAN
    shaped = values.reshape(N_CHAN, N_TILE, PH_DEV, N_CHAN, group_rows, MP)
    shaped = jnp.transpose(shaped, (3, 1, 0, 4, 2, 5))
    shaped = shaped.reshape(N_CHAN, N_TILE, CH_DEV, tile_rows, M)
    shaped = jnp.transpose(shaped, (0, 2, 1, 3, 4))
    return shaped.reshape(NCH, M, M)


def ladder_one(items):
    left, right, weight = items
    first = jnp.dot(left * weight[None, :], right, preferred_element_type=jnp.float32)
    second = jnp.dot(right * weight[None, :], left, preferred_element_type=jnp.float32)
    return first - second


def crossed_one(items):
    left, right, column_map, weights, occ_first, occ_second = items
    left_bar = (jnp.take(left, column_map, axis=1).astype(jnp.float32) * weights).astype(jnp.bfloat16)
    right_bar = (jnp.take(right, column_map, axis=1).astype(jnp.float32) * weights).astype(jnp.bfloat16)
    signs = (occ_first - occ_second).astype(jnp.bfloat16)
    crossed = jnp.dot(left_bar * signs[None, :], right_bar, preferred_element_type=jnp.float32)
    crossed = crossed - jnp.dot(right_bar * signs[None, :], left_bar, preferred_element_type=jnp.float32)
    inverse = jnp.argsort(column_map).astype(jnp.int32)
    return jnp.take(crossed * weights, inverse, axis=1).astype(jnp.bfloat16)


def reference(generator, hamiltonian, chan_sizes, pair_occupation, recoupled_occupation, recouple_map, recouple_weights):
    states = jnp.arange(M, dtype=jnp.int32)
    live_vec = states[None, :] < chan_sizes[:, None]
    live_mask = live_vec[:, :, None] & live_vec[:, None, :]
    zero = jnp.zeros((), jnp.bfloat16)
    eta_live = jnp.where(live_mask, generator, zero)
    gamma_live = jnp.where(live_mask, hamiltonian, zero)
    weight = ((1 - pair_occupation[0] - pair_occupation[1]) * live_vec.astype(jnp.int32)).astype(jnp.bfloat16)
    ladder = lax.map(ladder_one, (eta_live, gamma_live, weight))
    back_bar = lax.map(crossed_one, (to_recoupled(eta_live), to_recoupled(gamma_live), recouple_map, recouple_weights, recoupled_occupation[0], recoupled_occupation[1]))
    back = from_recoupled(back_bar)
    total = ladder + back.astype(jnp.float32)
    return jnp.where(live_mask, total, jnp.zeros((), jnp.float32)).astype(jnp.bfloat16)
```

```python
import functools

import jax
import jax.numpy as jnp
from jax import lax
from jax.experimental import pallas as pl
from jax.experimental.pallas import tpu as pltpu
from jax.sharding import PartitionSpec as P

MESH = pl.DeviceIdType.MESH
BF = jnp.bfloat16
F32 = jnp.float32
BLK = 128

ORDER = (0, 1, 7, 2, 6, 3, 5, 4)


def pairs_of(flip_ties):
    found = []
    for i in range(8):
        for j in range(i + 1, 8):
            a, b = ORDER[i], ORDER[j]
            if flip_ties and a + b == 8:
                a, b = b, a
            found.append((a, b))
    return found


def at128(index):
    return pl.ds(pl.multiple_of(index * BLK, BLK), BLK)


def kernel(
    n_chan,
    e_hbm,
    g_hbm,
    sizes,
    pocc,
    rocc,
    cmap,
    w_hbm,
    lad_out,
    back_out,
    e_m,
    g_m,
    rec_e,
    rec_g,
    e_full,
    g_full,
    ew,
    gw,
    lad_send,
    back_send,
    wts,
    onehot,
    e_bar,
    g_bar,
    wrow,
    load_sem,
    w_sem,
    own_sem,
    a2a_send,
    a2a_recv,
    gat_send,
    gat_recv,
    lad_ssem,
    lad_rsem,
    back_ssem,
    back_rsem,
):
    c = lax.axis_index("chan")
    t = lax.axis_index("tile")
    core = lax.rem(c, 2)
    group = 512 // n_chan

    load_e = pltpu.make_async_copy(e_hbm, e_m, load_sem.at[0])
    load_g = pltpu.make_async_copy(g_hbm, g_m, load_sem.at[1])
    load_e.start()
    load_g.start()
    load_w = pltpu.make_async_copy(w_hbm, wts, w_sem)
    load_w.start()

    barrier = pltpu.get_barrier_semaphore()

    @pl.loop(1, n_chan)
    def _(k):
        pl.semaphore_signal(barrier, inc=1, device_id=(c ^ k, t), device_id_type=MESH)

    @pl.loop(1, 8)
    def _(k):
        pl.semaphore_signal(barrier, inc=1, device_id=(c, lax.rem(t + k, 8)), device_id_type=MESH)

    cols = lax.broadcasted_iota(jnp.int32, (1, 1024), 1)
    rows = lax.broadcasted_iota(jnp.int32, (BLK, 1), 0) + t * BLK
    load_e.wait()
    load_g.wait()
    for h in range(4):
        size = sizes[h]
        col_live = (cols < size).astype(F32)
        row_live = (rows < size).astype(F32)
        wrow[h] = (1 - pocc[0, pl.ds(h, 1), :] - pocc[1, pl.ds(h, 1), :]).astype(F32) * col_live
        live = (row_live * col_live).astype(BF)
        e_m[h] = e_m[h] * live
        g_m[h] = g_m[h] * live

    pl.semaphore_wait(barrier, n_chan + 6)

    for h in range(4):
        owner = 2 * h + core
        delta = lax.rem(t - owner + 8, 8)
        far = jnp.minimum(delta, 8 - delta)

        def send(src, dst, which, j, h=h, owner=owner, delta=delta):
            pltpu.make_async_remote_copy(
                src_ref=src.at[h, :, at128(lax.rem(owner + j, 8))],
                dst_ref=dst.at[at128(delta), at128(j)],
                send_sem=gat_send,
                recv_sem=gat_recv.at[which],
                device_id=(c, owner),
                device_id_type=MESH,
            ).start()

        @pl.when(delta != 0)
        def _(send=send, far=far, delta=delta):
            send(e_m, e_full, 0, delta)
            send(g_m, g_full, 1, delta)

            @pl.when(delta < 4)
            def _():
                send(e_m, e_full, 0, 8 - delta)

            @pl.when(delta > 4)
            def _():
                send(g_m, g_full, 1, 8 - delta)

            @pl.loop(far + 1, 8 - far)
            def _(j):
                send(e_m, e_full, 0, j)
                send(g_m, g_full, 1, j)

    @pl.loop(1, n_chan)
    def _(k):
        s = c ^ k
        first = pl.multiple_of(lax.rem(s * group, BLK), group)
        mine = pl.ds(pl.multiple_of(c * group, group), group)
        for n, (src, dst) in enumerate(((e_m, rec_e), (g_m, rec_g))):
            pltpu.make_async_remote_copy(
                src_ref=src.at[(s * group) // BLK, pl.ds(first, group), :],
                dst_ref=dst.at[mine, :],
                send_sem=a2a_send,
                recv_sem=a2a_recv.at[n],
                device_id=(s, t),
                device_id_type=MESH,
            ).start()

    own_h = (c * group) // BLK
    own_rows = pl.ds(pl.multiple_of(lax.rem(c * group, BLK), group), group)
    own_place = pl.ds(pl.multiple_of(c * group, group), group)
    rec_e[own_place, :] = e_m[own_h, own_rows, :]
    rec_g[own_place, :] = g_m[own_h, own_rows, :]

    for q in range(2):
        spots = lax.broadcasted_iota(jnp.int32, (512, 512), 0)
        onehot[q] = (spots == cmap[pl.ds(q, 1), :]).astype(F32).astype(BF)

    is_owner = lax.rem(t, 2) == core

    @pl.when(is_owner)
    def _():
        h = t // 2
        for j in range(8):
            place = at128(lax.rem(t + j, 8))
            here = pl.ds(j * BLK, BLK)
            e_full[pl.ds(0, BLK), here] = e_m[h, :, place]
            g_full[pl.ds(0, BLK), here] = g_m[h, :, place]
        for n, full in enumerate((e_full, g_full)):
            landed = full.at[pl.ds(0, 28 * 16), :]
            pltpu.make_async_copy(landed, landed, gat_recv.at[n]).wait()
        for a, b in pairs_of(False):
            block = e_full[pl.ds(a * BLK, BLK), pl.ds(b * BLK, BLK)]
            e_full[pl.ds(b * BLK, BLK), pl.ds(a * BLK, BLK)] = -block.T
        for a, b in pairs_of(True):
            block = g_full[pl.ds(a * BLK, BLK), pl.ds(b * BLK, BLK)]
            g_full[pl.ds(b * BLK, BLK), pl.ds(a * BLK, BLK)] = block.T
        for j in range(8):
            here = pl.ds(j * BLK, BLK)
            weight = wrow[h, :, at128(lax.rem(t + j, 8))].astype(BF)
            ew[:, here] = e_full[:, here] * weight
            gw[:, here] = g_full[:, here] * weight

        @pl.loop(0, 4)
        def _(jj):
            half = pl.ds(pl.multiple_of(jj * 256, 256), 256)
            total = jnp.dot(ew[...], g_full[:, half], preferred_element_type=F32)
            total = total - jnp.dot(gw[...], e_full[:, half], preferred_element_type=F32)
            lad_send[:, half] = total.astype(BF)
            for i in (4, 3, 5, 2, 6, 1, 7):
                for m in range(2):
                    j = 2 * jj + m
                    pltpu.make_async_remote_copy(
                        src_ref=lad_send.at[pl.ds(i * BLK, BLK), at128(j)],
                        dst_ref=lad_out.at[h, :, at128(lax.rem(t + j, 8))],
                        send_sem=lad_ssem,
                        recv_sem=lad_rsem,
                        device_id=(c, lax.rem(t + i, 8)),
                        device_id_type=MESH,
                    ).start()
            for m in range(2):
                j = 2 * jj + m
                pltpu.make_async_copy(
                    lad_send.at[pl.ds(0, BLK), at128(j)],
                    lad_out.at[h, :, at128(lax.rem(t + j, 8))],
                    own_sem.at[0],
                ).start()

    load_w.wait()
    for n, rec in enumerate((rec_e, rec_g)):
        landed = rec.at[pl.ds(0, 512 - group), :]
        pltpu.make_async_copy(landed, landed, a2a_recv.at[n]).wait()

    @pl.loop(0, 2)
    def _(q):
        side = pl.ds(pl.multiple_of(q * 512, 512), 512)
        turn = onehot[q]
        scale = wts[q]
        e_bar[...] = (jnp.dot(rec_e[:, side], turn, preferred_element_type=F32) * scale).astype(BF)
        g_bar[...] = (jnp.dot(rec_g[:, side], turn, preferred_element_type=F32) * scale).astype(BF)
        signs = (rocc[0, pl.ds(q, 1), :] - rocc[1, pl.ds(q, 1), :]).astype(F32).astype(BF)
        crossed = jnp.dot(e_bar[...] * signs, g_bar[...], preferred_element_type=F32)
        crossed = crossed - jnp.dot(g_bar[...] * signs, e_bar[...], preferred_element_type=F32)
        scaled = (crossed * scale).astype(BF)
        back_send[:, side] = lax.dot_general(
            scaled, turn, (((1,), (1,)), ((), ())), preferred_element_type=F32
        ).astype(BF)

        @pl.loop(1, n_chan)
        def _(k):
            s = c ^ k
            pltpu.make_async_remote_copy(
                src_ref=back_send.at[pl.ds(pl.multiple_of(s * group, group), group), side],
                dst_ref=back_out.at[own_place, side],
                send_sem=back_ssem,
                recv_sem=back_rsem,
                device_id=(s, t),
                device_id_type=MESH,
            ).start()

    keep = pltpu.make_async_copy(back_send.at[own_place, :], back_out.at[own_place, :], own_sem.at[1])
    keep.start()

    def drain(ref, count, sem):
        piece = ref.at[pl.ds(0, count), :]
        pltpu.make_async_copy(piece, piece, sem).wait()

    for n in range(2):
        drain(rec_e, 512 - group, a2a_send)

    @pl.when(is_owner)
    def _():
        drain(lad_send, 20 * 16, gat_send)
        drain(lad_send, 7 * BLK, lad_ssem)
        drain(lad_send, BLK, own_sem.at[0])
        drain(lad_send, 3 * BLK, lad_rsem)

    @pl.when(jnp.logical_not(is_owner))
    def _():
        drain(lad_send, 36 * 16, gat_send)
        drain(lad_send, 4 * BLK, lad_rsem)

    keep.wait()
    drain(rec_e, 512 - group, back_ssem)
    drain(rec_e, 512 - group, back_rsem)


def exchange(n_chan, *args):
    vmem = pl.BlockSpec(memory_space=pltpu.VMEM)
    smem = pl.BlockSpec(memory_space=pltpu.SMEM)
    anywhere = pl.BlockSpec(memory_space=pl.ANY)
    dma = pltpu.SemaphoreType.DMA
    return pl.pallas_call(
        functools.partial(kernel, n_chan),
        name="commutator_exchange",
        out_shape=(
            jax.ShapeDtypeStruct((4, BLK, 1024), BF),
            jax.ShapeDtypeStruct((512, 1024), BF),
        ),
        in_specs=[anywhere, anywhere, smem, vmem, vmem, vmem, anywhere],
        out_specs=(anywhere, anywhere),
        scratch_shapes=[
            pltpu.VMEM((4, BLK, 1024), BF),
            pltpu.VMEM((4, BLK, 1024), BF),
            pltpu.VMEM((512, 1024), BF),
            pltpu.VMEM((512, 1024), BF),
            pltpu.VMEM((1024, 1024), BF),
            pltpu.VMEM((1024, 1024), BF),
            pltpu.VMEM((1024, 1024), BF),
            pltpu.VMEM((1024, 1024), BF),
            pltpu.VMEM((1024, 1024), BF),
            pltpu.VMEM((512, 1024), BF),
            pltpu.VMEM((2, 512, 512), F32),
            pltpu.VMEM((2, 512, 512), BF),
            pltpu.VMEM((512, 512), BF),
            pltpu.VMEM((512, 512), BF),
            pltpu.VMEM((4, 1, 1024), F32),
            dma((2,)),
            dma,
            dma((2,)),
            dma,
            dma((2,)),
            dma,
            dma((2,)),
            dma,
            dma,
            dma,
            dma,
        ],
        compiler_params=pltpu.CompilerParams(
            collective_id=0, has_side_effects=True, vmem_limit_bytes=56 * 1024 * 1024
        ),
    )(*args)


def per_device(
    n_chan,
    generator,
    hamiltonian,
    chan_sizes,
    pair_occupation,
    recoupled_occupation,
    recouple_map,
    recouple_weights,
):
    chan_count, tile_rows, states = generator.shape
    ladder, back = exchange(
        n_chan,
        generator,
        hamiltonian,
        chan_sizes,
        pair_occupation,
        recoupled_occupation,
        recouple_map,
        recouple_weights,
    )
    shape = (chan_count, tile_rows, states)
    sizes = chan_sizes[:, None, None]
    row = lax.axis_index("tile") * tile_rows + lax.broadcasted_iota(jnp.int32, shape, 1)
    column = lax.broadcasted_iota(jnp.int32, shape, 2)
    total = ladder.astype(F32) + back.reshape(shape).astype(F32)
    return jnp.where((row < sizes) & (column < sizes), total, jnp.zeros((), F32)).astype(BF)


def solution(mesh):
    return jax.shard_map(
        functools.partial(per_device, mesh.shape["chan"]),
        mesh=mesh,
        in_specs=(
            P("chan", "tile", None),
            P("chan", "tile", None),
            P("chan"),
            P(None, "chan", None),
            P(None, ("chan", "tile"), None),
            P(("chan", "tile"), None),
            P(("chan", "tile"), None, None),
        ),
        out_specs=P("chan", "tile", None),
        check_vma=False,
    )
```

```python
import functools

import jax
import jax.numpy as jnp
from jax import lax
from jax.experimental import pallas as pl
from jax.experimental.pallas import tpu as pltpu
from jax.sharding import PartitionSpec as P

MESH = pl.DeviceIdType.MESH
BF = jnp.bfloat16
F32 = jnp.float32
BLK = 128

ORDER = (0, 1, 7, 2, 6, 3, 5, 4)


def pairs_of(flip_ties):
    found = []
    for i in range(8):
        for j in range(i + 1, 8):
            a, b = ORDER[i], ORDER[j]
            if flip_ties and a + b == 8:
                a, b = b, a
            found.append((a, b))
    return found


def hops(move):
    return min(move[0], 4 - move[0]) + min(move[1], 4 - move[1])


def moves():
    listed = []
    everything = [(x, y, k) for y in range(4) for x in range(4) for k in range(2) if (x, y, k) != (0, 0, 0)]
    for far in (1, 2, 3, 4, 0):
        left = [m for m in everything if hops(m) == far]
        taken = []
        while left:
            recent = taken[-3:][::-1]
            cost = lambda m: sum(((m[0] == p[0]) + (m[1] == p[1])) * (3 - i) for i, p in enumerate(recent))
            taken.append(min(left, key=cost))
            left.remove(taken[-1])
        listed += taken
    return listed[::-1]


def dot_rows(a, b):
    return lax.dot_general(a, b, (((1,), (1,)), ((), ())), preferred_element_type=F32)


def at128(index):
    return pl.ds(pl.multiple_of(index * BLK, BLK), BLK)


def kernel(
    n_chan,
    e_hbm,
    g_hbm,
    sizes,
    pocc,
    rocc,
    cmap,
    w_hbm,
    lad_out,
    back_out,
    e_m,
    g_m,
    rec_e,
    rec_g,
    e_full,
    g_full,
    diag,
    lad_send,
    back_send,
    wts,
    onehot,
    e_bar,
    g_bar,
    wrow,
    load_sem,
    w_sem,
    own_sem,
    a2a_send,
    a2a_recv,
    gat_send,
    gat_recv,
    lad_ssem,
    lad_rsem,
    back_ssem,
    back_rsem,
):
    c = lax.axis_index("chan")
    t = lax.axis_index("tile")
    core = lax.rem(c, 2)
    group = 512 // n_chan

    def target(move):
        x, y, k = move
        return lax.rem(c // 8 + y, 4) * 8 + lax.rem(c // 2 + x, 4) * 2 + lax.rem(core + k, 2)

    load_e = pltpu.make_async_copy(e_hbm, e_m, load_sem.at[0])
    load_g = pltpu.make_async_copy(g_hbm, g_m, load_sem.at[1])
    load_e.start()
    load_g.start()
    load_w = pltpu.make_async_copy(w_hbm, wts, w_sem)
    load_w.start()

    barrier = pltpu.get_barrier_semaphore()

    @pl.loop(1, n_chan)
    def _(k):
        pl.semaphore_signal(barrier, inc=1, device_id=(c ^ k, t), device_id_type=MESH)

    @pl.loop(1, 8)
    def _(k):
        pl.semaphore_signal(barrier, inc=1, device_id=(c, lax.rem(t + k, 8)), device_id_type=MESH)

    cols = lax.broadcasted_iota(jnp.int32, (1, 1024), 1)
    rows = lax.broadcasted_iota(jnp.int32, (BLK, 1), 0) + t * BLK
    load_e.wait()
    load_g.wait()
    for h in range(4):
        size = sizes[h]
        col_live = (cols < size).astype(F32)
        row_live = (rows < size).astype(F32)
        wrow[h] = (1 - pocc[0, pl.ds(h, 1), :] - pocc[1, pl.ds(h, 1), :]).astype(F32) * col_live
        live = (row_live * col_live).astype(BF)
        e_m[h] = e_m[h] * live
        g_m[h] = g_m[h] * live

    pl.semaphore_wait(barrier, n_chan + 6)

    def gather(src, dst, which):
        for h in range(4):
            owner = 2 * h + core
            delta = lax.rem(t - owner + 8, 8)
            far = jnp.minimum(delta, 8 - delta)

            def send(j, h=h, owner=owner, delta=delta):
                pltpu.make_async_remote_copy(
                    src_ref=src.at[h, :, at128(lax.rem(owner + j, 8))],
                    dst_ref=dst.at[at128(delta), at128(j)],
                    send_sem=gat_send,
                    recv_sem=gat_recv.at[which],
                    device_id=(c, owner),
                    device_id_type=MESH,
                ).start()

            @pl.when(delta != 0)
            def _(send=send, far=far, delta=delta):
                send(delta)

                @pl.when(delta > 4 if which else delta < 4)
                def _():
                    send(8 - delta)

                @pl.loop(far + 1, 8 - far)
                def _(j):
                    send(j)

    gather(e_m, e_full, 0)

    own_place = pl.ds(pl.multiple_of(c * group, group), group)
    for move in moves():
        s = target(move)
        first = pl.multiple_of(lax.rem(s * group, BLK), group)
        for n, (src, dst) in enumerate(((e_m, rec_e), (g_m, rec_g))):
            pltpu.make_async_remote_copy(
                src_ref=src.at[(s * group) // BLK, pl.ds(first, group), :],
                dst_ref=dst.at[own_place, :],
                send_sem=a2a_send,
                recv_sem=a2a_recv.at[n],
                device_id=(s, t),
                device_id_type=MESH,
            ).start()

    gather(g_m, g_full, 1)

    own_h = (c * group) // BLK
    own_rows = pl.ds(pl.multiple_of(lax.rem(c * group, BLK), group), group)
    rec_e[own_place, :] = e_m[own_h, own_rows, :]
    rec_g[own_place, :] = g_m[own_h, own_rows, :]

    for q in range(2):
        spots = lax.broadcasted_iota(jnp.int32, (512, 512), 0)
        onehot[q] = (spots == cmap[pl.ds(q, 1), :]).astype(F32).astype(BF)

    for h in range(4):
        weight = wrow[h].astype(BF)
        mine = dot_rows(e_m[h] * weight, g_m[h]) + dot_rows(g_m[h] * weight, e_m[h])
        diag[h] = mine.astype(BF)
        pltpu.make_async_copy(diag.at[h], lad_out.at[h, :, at128(t)], own_sem.at[2]).start()

    is_owner = lax.rem(t, 2) == core

    @pl.when(is_owner)
    def _():
        h = t // 2
        for j in range(8):
            place = at128(lax.rem(t + j, 8))
            here = pl.ds(j * BLK, BLK)
            e_full[pl.ds(0, BLK), here] = e_m[h, :, place]
            g_full[pl.ds(0, BLK), here] = g_m[h, :, place]

        def arrive(full, which):
            landed = full.at[pl.ds(0, 28 * 16), :]
            pltpu.make_async_copy(landed, landed, gat_recv.at[which]).wait()
            for a, b in pairs_of(which):
                block = full[pl.ds(a * BLK, BLK), pl.ds(b * BLK, BLK)].T
                full[pl.ds(b * BLK, BLK), pl.ds(a * BLK, BLK)] = block if which else -block

        arrive(e_full, 0)
        for j in range(8):
            here = pl.ds(j * BLK, BLK)
            weight = wrow[h, :, at128(lax.rem(t + j, 8))].astype(BF)
            e_full[:, here] = e_full[:, here] * weight
        arrive(g_full, 1)

        @pl.loop(0, 4)
        def _(jj):
            half = pl.ds(pl.multiple_of(jj * 256, 256), 256)
            total = jnp.dot(e_full[...], g_full[:, half], preferred_element_type=F32)
            total = total + dot_rows(g_full[...], e_full[half, :])
            lad_send[:, half] = total.astype(BF)
            for i in (4, 3, 5, 2, 6, 1, 7):
                for m in range(2):
                    j = 2 * jj + m

                    @pl.when(j != i)
                    def _(i=i, j=j):
                        pltpu.make_async_remote_copy(
                            src_ref=lad_send.at[pl.ds(i * BLK, BLK), at128(j)],
                            dst_ref=lad_out.at[h, :, at128(lax.rem(t + j, 8))],
                            send_sem=lad_ssem,
                            recv_sem=lad_rsem,
                            device_id=(c, lax.rem(t + i, 8)),
                            device_id_type=MESH,
                        ).start()

            for m in range(2):
                j = 2 * jj + m

                @pl.when(j != 0)
                def _(j=j):
                    pltpu.make_async_copy(
                        lad_send.at[pl.ds(0, BLK), at128(j)],
                        lad_out.at[h, :, at128(lax.rem(t + j, 8))],
                        own_sem.at[0],
                    ).start()

    load_w.wait()
    for n, rec in enumerate((rec_e, rec_g)):
        landed = rec.at[pl.ds(0, 512 - group), :]
        pltpu.make_async_copy(landed, landed, a2a_recv.at[n]).wait()

    @pl.loop(0, 2)
    def _(q):
        side = pl.ds(pl.multiple_of(q * 512, 512), 512)
        turn = onehot[q]
        scale = wts[q]
        e_bar[...] = (jnp.dot(rec_e[:, side], turn, preferred_element_type=F32) * scale).astype(BF)
        g_bar[...] = (jnp.dot(rec_g[:, side], turn, preferred_element_type=F32) * scale).astype(BF)
        signs = (rocc[0, pl.ds(q, 1), :] - rocc[1, pl.ds(q, 1), :]).astype(F32).astype(BF)
        crossed = jnp.dot(e_bar[...] * signs, g_bar[...], preferred_element_type=F32)
        crossed = crossed - jnp.dot(g_bar[...] * signs, e_bar[...], preferred_element_type=F32)
        scaled = (crossed * scale).astype(BF)
        back_send[:, side] = dot_rows(scaled, turn).astype(BF)
        for move in moves():
            s = target(move)
            pltpu.make_async_remote_copy(
                src_ref=back_send.at[pl.ds(pl.multiple_of(s * group, group), group), side],
                dst_ref=back_out.at[own_place, side],
                send_sem=back_ssem,
                recv_sem=back_rsem,
                device_id=(s, t),
                device_id_type=MESH,
            ).start()

    keep = pltpu.make_async_copy(back_send.at[own_place, :], back_out.at[own_place, :], own_sem.at[1])
    keep.start()

    def drain(ref, count, sem):
        piece = ref.at[pl.ds(0, count), :]
        pltpu.make_async_copy(piece, piece, sem).wait()

    for n in range(2):
        drain(rec_e, 512 - group, a2a_send)

    @pl.when(is_owner)
    def _():
        drain(lad_send, 20 * 16, gat_send)
        drain(lad_send, 49 * 16, lad_ssem)
        drain(lad_send, 7 * 16, own_sem.at[0])
        drain(lad_send, 3 * 7 * 16, lad_rsem)

    @pl.when(jnp.logical_not(is_owner))
    def _():
        drain(lad_send, 36 * 16, gat_send)
        drain(lad_send, 4 * 7 * 16, lad_rsem)

    keep.wait()
    drain(lad_send, 4 * 16, own_sem.at[2])
    drain(rec_e, 512 - group, back_ssem)
    drain(rec_e, 512 - group, back_rsem)


def exchange(n_chan, *args):
    vmem = pl.BlockSpec(memory_space=pltpu.VMEM)
    smem = pl.BlockSpec(memory_space=pltpu.SMEM)
    anywhere = pl.BlockSpec(memory_space=pl.ANY)
    dma = pltpu.SemaphoreType.DMA
    return pl.pallas_call(
        functools.partial(kernel, n_chan),
        name="commutator_exchange",
        out_shape=(
            jax.ShapeDtypeStruct((4, BLK, 1024), BF),
            jax.ShapeDtypeStruct((512, 1024), BF),
        ),
        in_specs=[anywhere, anywhere, smem, vmem, vmem, vmem, anywhere],
        out_specs=(anywhere, anywhere),
        scratch_shapes=[
            pltpu.VMEM((4, BLK, 1024), BF),
            pltpu.VMEM((4, BLK, 1024), BF),
            pltpu.VMEM((512, 1024), BF),
            pltpu.VMEM((512, 1024), BF),
            pltpu.VMEM((1024, 1024), BF),
            pltpu.VMEM((1024, 1024), BF),
            pltpu.VMEM((4, BLK, BLK), BF),
            pltpu.VMEM((1024, 1024), BF),
            pltpu.VMEM((512, 1024), BF),
            pltpu.VMEM((2, 512, 512), F32),
            pltpu.VMEM((2, 512, 512), BF),
            pltpu.VMEM((512, 512), BF),
            pltpu.VMEM((512, 512), BF),
            pltpu.VMEM((4, 1, 1024), F32),
            dma((2,)),
            dma,
            dma((3,)),
            dma,
            dma((2,)),
            dma,
            dma((2,)),
            dma,
            dma,
            dma,
            dma,
        ],
        compiler_params=pltpu.CompilerParams(
            collective_id=0, has_side_effects=True, vmem_limit_bytes=56 * 1024 * 1024
        ),
    )(*args)


def combine_kernel(sizes, ladder, back, out):
    h = pl.program_id(0)
    size = sizes[h]
    row = lax.broadcasted_iota(jnp.int32, (BLK, 1), 0) + lax.axis_index("tile") * BLK
    column = lax.broadcasted_iota(jnp.int32, (1, 1024), 1)
    live = (row < size).astype(F32) * (column < size).astype(F32)
    total = ladder[...].astype(F32) + back[...].astype(F32)
    out[...] = jnp.where(live > 0, total, 0.0).astype(BF)


def combine(sizes, ladder, back):
    piece = pl.BlockSpec((None, BLK, 1024), lambda h: (h, 0, 0))
    return pl.pallas_call(
        combine_kernel,
        name="combine",
        grid=(4,),
        out_shape=jax.ShapeDtypeStruct(ladder.shape, BF),
        in_specs=[pl.BlockSpec(memory_space=pltpu.SMEM), piece, piece],
        out_specs=piece,
    )(sizes, ladder, back)


def per_device(
    n_chan,
    generator,
    hamiltonian,
    chan_sizes,
    pair_occupation,
    recoupled_occupation,
    recouple_map,
    recouple_weights,
):
    chan_count, tile_rows, states = generator.shape
    ladder, back = exchange(
        n_chan,
        generator,
        hamiltonian,
        chan_sizes,
        pair_occupation,
        recoupled_occupation,
        recouple_map,
        recouple_weights,
    )
    return combine(chan_sizes, ladder, back.reshape(chan_count, tile_rows, states))


def solution(mesh):
    return jax.shard_map(
        functools.partial(per_device, mesh.shape["chan"]),
        mesh=mesh,
        in_specs=(
            P("chan", "tile", None),
            P("chan", "tile", None),
            P("chan"),
            P(None, "chan", None),
            P(None, ("chan", "tile"), None),
            P(("chan", "tile"), None),
            P(("chan", "tile"), None, None),
        ),
        out_specs=P("chan", "tile", None),
        check_vma=False,
    )
```

```python
import functools

import jax
import jax.numpy as jnp
from jax import lax
from jax.experimental import pallas as pl
from jax.experimental.pallas import tpu as pltpu
from jax.sharding import PartitionSpec as P

MESH = pl.DeviceIdType.MESH
BF = jnp.bfloat16
F32 = jnp.float32
BLK = 128
VMEM_BYTES = 30 * 1024 * 1024

ORDER = (0, 1, 7, 2, 6, 3, 5, 4)


def pairs_of(flip_ties):
    found = []
    for i in range(8):
        for j in range(i + 1, 8):
            a, b = ORDER[i], ORDER[j]
            if flip_ties and a + b == 8:
                a, b = b, a
            found.append((a, b))
    return found


def hops(move):
    return min(move[0], 4 - move[0]) + min(move[1], 4 - move[1])


def moves():
    listed = []
    everything = [(x, y, k) for y in range(4) for x in range(4) for k in range(2) if (x, y, k) != (0, 0, 0)]
    for far in (1, 2, 3, 4, 0):
        left = [m for m in everything if hops(m) == far]
        taken = []
        while left:
            recent = taken[-3:][::-1]
            cost = lambda m: sum(((m[0] == p[0]) + (m[1] == p[1])) * (3 - i) for i, p in enumerate(recent))
            taken.append(min(left, key=cost))
            left.remove(taken[-1])
        listed += taken
    return listed[::-1]


def dot_rows(a, b):
    return lax.dot_general(a, b, (((1,), (1,)), ((), ())), preferred_element_type=F32)


def at128(index):
    return pl.ds(pl.multiple_of(index * BLK, BLK), BLK)


def kernel(
    n_chan,
    e_hbm,
    g_hbm,
    sizes,
    pocc_hbm,
    rocc_hbm,
    cmap_hbm,
    w_hbm,
    lad_out,
    back_out,
    e_m,
    g_m,
    rec_e,
    rec_g,
    e_full,
    g_full,
    diag,
    lad_send,
    back_send,
    wts,
    onehot,
    e_bar,
    g_bar,
    wrow,
    pocc,
    rocc,
    cmap,
    load_sem,
    w_sem,
    own_sem,
    a2a_send,
    a2a_recv,
    gat_send,
    gat_recv,
    lad_ssem,
    lad_rsem,
    back_ssem,
    back_rsem,
):
    c = lax.axis_index("chan")
    t = lax.axis_index("tile")
    core = lax.rem(c, 2)
    group = 512 // n_chan

    def target(move):
        x, y, k = move
        return lax.rem(c // 8 + y, 4) * 8 + lax.rem(c // 2 + x, 4) * 2 + lax.rem(core + k, 2)

    load_e = pltpu.make_async_copy(e_hbm, e_m, load_sem.at[0])
    load_g = pltpu.make_async_copy(g_hbm, g_m, load_sem.at[1])
    load_e.start()
    load_g.start()
    small = [
        pltpu.make_async_copy(src, dst, load_sem.at[n])
        for n, (src, dst) in enumerate(((pocc_hbm, pocc), (cmap_hbm, cmap), (rocc_hbm, rocc)), 2)
    ]
    for load in small:
        load.start()
    load_w = pltpu.make_async_copy(w_hbm, wts, w_sem)
    load_w.start()

    barrier = pltpu.get_barrier_semaphore()

    @pl.loop(1, n_chan)
    def _(k):
        pl.semaphore_signal(barrier, inc=1, device_id=(c ^ k, t), device_id_type=MESH)

    @pl.loop(1, 8)
    def _(k):
        pl.semaphore_signal(barrier, inc=1, device_id=(c, lax.rem(t + k, 8)), device_id_type=MESH)

    cols = lax.broadcasted_iota(jnp.int32, (1, 1024), 1)
    rows = lax.broadcasted_iota(jnp.int32, (BLK, 1), 0) + t * BLK
    load_e.wait()
    load_g.wait()
    small[0].wait()
    for h in range(4):
        size = sizes[h]
        col_live = (cols < size).astype(F32)
        row_live = (rows < size).astype(F32)
        wrow[h] = (1 - pocc[0, pl.ds(h, 1), :] - pocc[1, pl.ds(h, 1), :]).astype(F32) * col_live
        live = (row_live * col_live).astype(BF)
        e_m[h] = e_m[h] * live
        g_m[h] = g_m[h] * live

    pl.semaphore_wait(barrier, n_chan + 6)

    def gather(src, dst, which, phase):
        for h in (2 * phase, 2 * phase + 1):
            owner = 4 * (h % 2) + phase + 2 * core
            delta = lax.rem(t - owner + 8, 8)
            far = jnp.minimum(delta, 8 - delta)

            def send(j, h=h, owner=owner, delta=delta):
                pltpu.make_async_remote_copy(
                    src_ref=src.at[h, :, at128(lax.rem(owner + j, 8))],
                    dst_ref=dst.at[at128(delta), at128(j)],
                    send_sem=gat_send,
                    recv_sem=gat_recv.at[which],
                    device_id=(c, owner),
                    device_id_type=MESH,
                ).start()

            @pl.when(delta != 0)
            def _(send=send, far=far, delta=delta):
                send(delta)

                @pl.when(delta > 4 if which else delta < 4)
                def _():
                    send(8 - delta)

                @pl.loop(far + 1, 8 - far)
                def _(j):
                    send(j)

    gather(e_m, e_full, 0, 0)
    gather(g_m, g_full, 1, 0)

    own_place = pl.ds(pl.multiple_of(c * group, group), group)
    for move in moves():
        s = target(move)
        first = pl.multiple_of(lax.rem(s * group, BLK), group)
        for n, (src, dst) in enumerate(((e_m, rec_e), (g_m, rec_g))):
            pltpu.make_async_remote_copy(
                src_ref=src.at[(s * group) // BLK, pl.ds(first, group), :],
                dst_ref=dst.at[own_place, :],
                send_sem=a2a_send,
                recv_sem=a2a_recv.at[n],
                device_id=(s, t),
                device_id_type=MESH,
            ).start()

    gather(e_m, e_full, 0, 1)
    gather(g_m, g_full, 1, 1)

    own_h = (c * group) // BLK
    own_rows = pl.ds(pl.multiple_of(lax.rem(c * group, BLK), group), group)
    rec_e[own_place, :] = e_m[own_h, own_rows, :]
    rec_g[own_place, :] = g_m[own_h, own_rows, :]

    small[1].wait()
    small[2].wait()
    for q in range(2):
        spots = lax.broadcasted_iota(jnp.int32, (512, 512), 0)
        onehot[q] = (spots == cmap[pl.ds(q, 1), :]).astype(F32).astype(BF)

    for h in range(4):
        weight = wrow[h].astype(BF)
        mine = dot_rows(e_m[h] * weight, g_m[h]) + dot_rows(g_m[h] * weight, e_m[h])
        diag[h] = mine.astype(BF)
        pltpu.make_async_copy(diag.at[h], lad_out.at[h, :, at128(t)], own_sem.at[2]).start()

    is_owner = lax.rem(t // 2, 2) == core

    @pl.when(is_owner)
    def _():
        h = 2 * lax.rem(t, 2) + t // 4
        for j in range(8):
            place = at128(lax.rem(t + j, 8))
            here = pl.ds(j * BLK, BLK)
            e_full[pl.ds(0, BLK), here] = e_m[h, :, place]
            g_full[pl.ds(0, BLK), here] = g_m[h, :, place]

        def arrive(full, which):
            landed = full.at[pl.ds(0, 28 * 16), :]
            pltpu.make_async_copy(landed, landed, gat_recv.at[which]).wait()
            for a, b in pairs_of(which):
                block = full[pl.ds(a * BLK, BLK), pl.ds(b * BLK, BLK)].T
                full[pl.ds(b * BLK, BLK), pl.ds(a * BLK, BLK)] = block if which else -block

        arrive(e_full, 0)
        for j in range(8):
            here = pl.ds(j * BLK, BLK)
            weight = wrow[h, :, at128(lax.rem(t + j, 8))].astype(BF)
            e_full[:, here] = e_full[:, here] * weight
        arrive(g_full, 1)

        @pl.loop(0, 4)
        def _(jj):
            half = pl.ds(pl.multiple_of(jj * 256, 256), 256)
            total = jnp.dot(e_full[...], g_full[:, half], preferred_element_type=F32)
            total = total + dot_rows(g_full[...], e_full[half, :])
            lad_send[:, half] = total.astype(BF)
            for i in (4, 3, 5, 2, 6, 1, 7):
                for m in range(2):
                    j = 2 * jj + m

                    @pl.when(j != i)
                    def _(i=i, j=j):
                        pltpu.make_async_remote_copy(
                            src_ref=lad_send.at[pl.ds(i * BLK, BLK), at128(j)],
                            dst_ref=lad_out.at[h, :, at128(lax.rem(t + j, 8))],
                            send_sem=lad_ssem,
                            recv_sem=lad_rsem,
                            device_id=(c, lax.rem(t + i, 8)),
                            device_id_type=MESH,
                        ).start()

            for m in range(2):
                j = 2 * jj + m

                @pl.when(j != 0)
                def _(j=j):
                    pltpu.make_async_copy(
                        lad_send.at[pl.ds(0, BLK), at128(j)],
                        lad_out.at[h, :, at128(lax.rem(t + j, 8))],
                        own_sem.at[0],
                    ).start()

    load_w.wait()
    for n, rec in enumerate((rec_e, rec_g)):
        landed = rec.at[pl.ds(0, 512 - group), :]
        pltpu.make_async_copy(landed, landed, a2a_recv.at[n]).wait()

    @pl.loop(0, 2)
    def _(q):
        side = pl.ds(pl.multiple_of(q * 512, 512), 512)
        turn = onehot[q]
        scale = wts[q]
        e_bar[...] = (jnp.dot(rec_e[:, side], turn, preferred_element_type=F32) * scale).astype(BF)
        g_bar[...] = (jnp.dot(rec_g[:, side], turn, preferred_element_type=F32) * scale).astype(BF)
        signs = (rocc[0, pl.ds(q, 1), :] - rocc[1, pl.ds(q, 1), :]).astype(F32).astype(BF)
        crossed = jnp.dot(e_bar[...] * signs, g_bar[...], preferred_element_type=F32)
        crossed = crossed - jnp.dot(g_bar[...] * signs, e_bar[...], preferred_element_type=F32)
        scaled = (crossed * scale).astype(BF)
        back_send[:, side] = dot_rows(scaled, turn).astype(BF)
        for move in moves():
            s = target(move)
            pltpu.make_async_remote_copy(
                src_ref=back_send.at[pl.ds(pl.multiple_of(s * group, group), group), side],
                dst_ref=back_out.at[own_place, side],
                send_sem=back_ssem,
                recv_sem=back_rsem,
                device_id=(s, t),
                device_id_type=MESH,
            ).start()

    keep = pltpu.make_async_copy(back_send.at[own_place, :], back_out.at[own_place, :], own_sem.at[1])
    keep.start()

    def drain(ref, count, sem):
        piece = ref.at[pl.ds(0, count), :]
        pltpu.make_async_copy(piece, piece, sem).wait()

    for n in range(2):
        drain(rec_e, 512 - group, a2a_send)

    @pl.when(is_owner)
    def _():
        drain(lad_send, 20 * 16, gat_send)
        drain(lad_send, 49 * 16, lad_ssem)
        drain(lad_send, 7 * 16, own_sem.at[0])
        drain(lad_send, 3 * 7 * 16, lad_rsem)

    @pl.when(jnp.logical_not(is_owner))
    def _():
        drain(lad_send, 36 * 16, gat_send)
        drain(lad_send, 4 * 7 * 16, lad_rsem)

    keep.wait()
    drain(lad_send, 4 * 16, own_sem.at[2])
    drain(rec_e, 512 - group, back_ssem)
    drain(rec_e, 512 - group, back_rsem)


def exchange(n_chan, *args):
    far = pl.BlockSpec(memory_space=pltpu.HBM)
    smem = pl.BlockSpec(memory_space=pltpu.SMEM)
    anywhere = pl.BlockSpec(memory_space=pl.ANY)
    dma = pltpu.SemaphoreType.DMA
    return pl.pallas_call(
        functools.partial(kernel, n_chan),
        name="commutator_exchange",
        out_shape=(
            jax.ShapeDtypeStruct((4, BLK, 1024), BF),
            jax.ShapeDtypeStruct((512, 1024), BF),
        ),
        in_specs=[far, far, smem, far, far, far, far],
        out_specs=(anywhere, anywhere),
        scratch_shapes=[
            pltpu.VMEM((4, BLK, 1024), BF),
            pltpu.VMEM((4, BLK, 1024), BF),
            pltpu.VMEM((512, 1024), BF),
            pltpu.VMEM((512, 1024), BF),
            pltpu.VMEM((1024, 1024), BF),
            pltpu.VMEM((1024, 1024), BF),
            pltpu.VMEM((4, BLK, BLK), BF),
            pltpu.VMEM((1024, 1024), BF),
            pltpu.VMEM((512, 1024), BF),
            pltpu.VMEM((2, 512, 512), F32),
            pltpu.VMEM((2, 512, 512), BF),
            pltpu.VMEM((512, 512), BF),
            pltpu.VMEM((512, 512), BF),
            pltpu.VMEM((4, 1, 1024), F32),
            pltpu.VMEM((2, 4, 1024), jnp.int32),
            pltpu.VMEM((2, 2, 512), jnp.int32),
            pltpu.VMEM((2, 512), jnp.int32),
            dma((5,)),
            dma,
            dma((3,)),
            dma,
            dma((2,)),
            dma,
            dma((2,)),
            dma,
            dma,
            dma,
            dma,
        ],
        compiler_params=pltpu.CompilerParams(
            collective_id=0, has_side_effects=True, vmem_limit_bytes=VMEM_BYTES
        ),
    )(*[pltpu.with_memory_space_constraint(a, pltpu.HBM) for a in args])


def per_device(
    n_chan,
    generator,
    hamiltonian,
    chan_sizes,
    pair_occupation,
    recoupled_occupation,
    recouple_map,
    recouple_weights,
):
    chan_count, tile_rows, states = generator.shape
    ladder, back = exchange(
        n_chan,
        generator,
        hamiltonian,
        chan_sizes,
        pair_occupation,
        recoupled_occupation,
        recouple_map,
        recouple_weights,
    )
    shape = (chan_count, tile_rows, states)
    sizes = chan_sizes[:, None, None]
    row = lax.axis_index("tile") * tile_rows + lax.broadcasted_iota(jnp.int32, shape, 1)
    column = lax.broadcasted_iota(jnp.int32, shape, 2)
    total = ladder.astype(F32) + back.reshape(shape).astype(F32)
    return jnp.where((row < sizes) & (column < sizes), total, jnp.zeros((), F32)).astype(BF)


def solution(mesh):
    return jax.shard_map(
        functools.partial(per_device, mesh.shape["chan"]),
        mesh=mesh,
        in_specs=(
            P("chan", "tile", None),
            P("chan", "tile", None),
            P("chan"),
            P(None, "chan", None),
            P(None, ("chan", "tile"), None),
            P(("chan", "tile"), None),
            P(("chan", "tile"), None, None),
        ),
        out_specs=P("chan", "tile", None),
        check_vma=False,
    )
```

```python
import functools

import jax
import jax.numpy as jnp
from jax import lax
from jax.experimental import pallas as pl
from jax.experimental.pallas import tpu as pltpu
from jax.sharding import PartitionSpec as P

MESH = pl.DeviceIdType.MESH
BF = jnp.bfloat16
F32 = jnp.float32
BLK = 128
VMEM_BYTES = 30 * 1024 * 1024

ORDER = (0, 1, 7, 2, 6, 3, 5, 4)


def pairs_of(flip_ties):
    found = []
    for i in range(8):
        for j in range(i + 1, 8):
            a, b = ORDER[i], ORDER[j]
            if flip_ties and a + b == 8:
                a, b = b, a
            found.append((a, b))
    return found


def hops(move):
    return min(move[0], 4 - move[0]) + min(move[1], 4 - move[1])


def moves():
    listed = []
    everything = [(x, y, k) for y in range(4) for x in range(4) for k in range(2) if (x, y, k) != (0, 0, 0)]
    for far in (1, 2, 3, 4, 0):
        left = [m for m in everything if hops(m) == far]
        taken = []
        while left:
            recent = taken[-3:][::-1]
            cost = lambda m: sum(((m[0] == p[0]) + (m[1] == p[1])) * (3 - i) for i, p in enumerate(recent))
            taken.append(min(left, key=cost))
            left.remove(taken[-1])
        listed += taken
    return listed[::-1]


def dot_rows(a, b):
    return lax.dot_general(a, b, (((1,), (1,)), ((), ())), preferred_element_type=F32)


def at128(index):
    return pl.ds(pl.multiple_of(index * BLK, BLK), BLK)


def kernel(
    n_chan,
    e_hbm,
    g_hbm,
    sizes,
    pocc_hbm,
    rocc_hbm,
    cmap_hbm,
    w_hbm,
    lad_out,
    back_out,
    e_m,
    g_m,
    rec_e,
    rec_g,
    e_full,
    g_full,
    diag,
    lad_send,
    back_send,
    wts,
    onehot,
    e_bar,
    g_bar,
    wrow,
    pocc,
    rocc,
    cmap,
    held,
    turned,
    load_sem,
    w_sem,
    own_sem,
    a2a_send,
    a2a_recv,
    gat_send,
    gat_recv,
    lad_ssem,
    lad_rsem,
    back_ssem,
    back_rsem,
    held_rsem,
    pass_ssem,
    pass_own,
):
    c = lax.axis_index("chan")
    t = lax.axis_index("tile")
    core = lax.rem(c, 2)
    group = 512 // n_chan

    def target(move):
        x, y, k = move
        return lax.rem(c // 8 + y, 4) * 8 + lax.rem(c // 2 + x, 4) * 2 + lax.rem(core + k, 2)

    load_e = pltpu.make_async_copy(e_hbm, e_m, load_sem.at[0])
    load_g = pltpu.make_async_copy(g_hbm, g_m, load_sem.at[1])
    load_e.start()
    load_g.start()
    small = [
        pltpu.make_async_copy(src, dst, load_sem.at[n])
        for n, (src, dst) in enumerate(((pocc_hbm, pocc), (cmap_hbm, cmap), (rocc_hbm, rocc)), 2)
    ]
    for load in small:
        load.start()
    load_w = pltpu.make_async_copy(w_hbm, wts, w_sem)
    load_w.start()

    barrier = pltpu.get_barrier_semaphore()

    @pl.loop(1, n_chan)
    def _(k):
        pl.semaphore_signal(barrier, inc=1, device_id=(c ^ k, t), device_id_type=MESH)

    @pl.loop(1, 8)
    def _(k):
        pl.semaphore_signal(barrier, inc=1, device_id=(c, lax.rem(t + k, 8)), device_id_type=MESH)

    cols = lax.broadcasted_iota(jnp.int32, (1, 1024), 1)
    rows = lax.broadcasted_iota(jnp.int32, (BLK, 1), 0) + t * BLK
    load_e.wait()
    load_g.wait()
    small[0].wait()
    for h in range(4):
        size = sizes[h]
        col_live = (cols < size).astype(F32)
        row_live = (rows < size).astype(F32)
        wrow[h] = (1 - pocc[0, pl.ds(h, 1), :] - pocc[1, pl.ds(h, 1), :]).astype(F32) * col_live
        live = (row_live * col_live).astype(BF)
        e_m[h] = e_m[h] * live
        g_m[h] = g_m[h] * live

    pl.semaphore_wait(barrier, n_chan + 6)

    def gather(src, dst, which, phase):
        for h in (2 * phase, 2 * phase + 1):
            owner = 4 * (h % 2) + phase + 2 * core
            delta = lax.rem(t - owner + 8, 8)
            far = jnp.minimum(delta, 8 - delta)

            def send(j, h=h, owner=owner, delta=delta):
                pltpu.make_async_remote_copy(
                    src_ref=src.at[h, :, at128(lax.rem(owner + j, 8))],
                    dst_ref=dst.at[at128(delta), at128(j)],
                    send_sem=gat_send,
                    recv_sem=gat_recv.at[which],
                    device_id=(c, owner),
                    device_id_type=MESH,
                ).start()

            @pl.when(delta != 0)
            def _(send=send, far=far, delta=delta):
                send(delta)

                @pl.when(delta > 4 if which else delta < 4)
                def _():
                    send(8 - delta)

                @pl.loop(far + 1, 8 - far)
                def _(j):
                    send(j)

    gather(e_m, e_full, 0, 0)
    gather(e_m, e_full, 0, 1)
    gather(g_m, g_full, 1, 0)

    own_place = pl.ds(pl.multiple_of(c * group, group), group)

    @pl.loop(0, 2)
    def _(q):
        side = pl.ds(pl.multiple_of(q * 512, 512), 512)
        for move in moves():
            s = target(move)
            first = pl.multiple_of(lax.rem(s * group, BLK), group)
            for n, (src, dst) in enumerate(((e_m, rec_e), (g_m, rec_g))):
                pltpu.make_async_remote_copy(
                    src_ref=src.at[(s * group) // BLK, pl.ds(first, group), side],
                    dst_ref=dst.at[own_place, side],
                    send_sem=a2a_send,
                    recv_sem=a2a_recv.at[q, n],
                    device_id=(s, t),
                    device_id_type=MESH,
                ).start()

    gather(g_m, g_full, 1, 1)

    own_h = (c * group) // BLK
    own_rows = pl.ds(pl.multiple_of(lax.rem(c * group, BLK), group), group)
    rec_e[own_place, :] = e_m[own_h, own_rows, :]
    rec_g[own_place, :] = g_m[own_h, own_rows, :]

    small[1].wait()
    small[2].wait()
    for q in range(2):
        spots = lax.broadcasted_iota(jnp.int32, (512, 512), 0)
        onehot[q] = (spots == cmap[pl.ds(q, 1), :]).astype(F32).astype(BF)

    for h in range(4):
        weight = wrow[h].astype(BF)
        mine = dot_rows(e_m[h] * weight, g_m[h]) + dot_rows(g_m[h] * weight, e_m[h])
        diag[h] = mine.astype(BF)
        pltpu.make_async_copy(diag.at[h], lad_out.at[h, :, at128(t)], own_sem.at[2]).start()

    is_owner = lax.rem(t // 2, 2) == core
    own = 2 * lax.rem(t, 2) + t // 4

    def arrive(full, which):
        landed = full.at[pl.ds(0, 28 * 16), :]
        pltpu.make_async_copy(landed, landed, gat_recv.at[which]).wait()
        for a, b in pairs_of(which):
            block = full[pl.ds(a * BLK, BLK), pl.ds(b * BLK, BLK)].T
            full[pl.ds(b * BLK, BLK), pl.ds(a * BLK, BLK)] = block if which else -block

    @pl.when(is_owner)
    def _():
        for j in range(8):
            place = at128(lax.rem(t + j, 8))
            here = pl.ds(j * BLK, BLK)
            e_full[pl.ds(0, BLK), here] = e_m[own, :, place]
            g_full[pl.ds(0, BLK), here] = g_m[own, :, place]
        arrive(e_full, 0)
        for j in range(8):
            here = pl.ds(j * BLK, BLK)
            weight = wrow[own, :, at128(lax.rem(t + j, 8))].astype(BF)
            e_full[:, here] = e_full[:, here] * weight

    def cross(q):
        side = pl.ds(q * 512, 512)
        for n, rec in enumerate((rec_e, rec_g)):
            landed = rec.at[pl.ds(0, 512 - group), side]
            pltpu.make_async_copy(landed, landed, a2a_recv.at[q, n]).wait()
        turn = onehot[q]
        scale = wts[q]
        e_bar[...] = (jnp.dot(rec_e[:, side], turn, preferred_element_type=F32) * scale).astype(BF)
        g_bar[...] = (jnp.dot(rec_g[:, side], turn, preferred_element_type=F32) * scale).astype(BF)
        signs = (rocc[0, pl.ds(q, 1), :] - rocc[1, pl.ds(q, 1), :]).astype(F32).astype(BF)
        crossed = jnp.dot(e_bar[...] * signs, g_bar[...], preferred_element_type=F32)
        crossed = crossed - jnp.dot(g_bar[...] * signs, e_bar[...], preferred_element_type=F32)
        scaled = (crossed * scale).astype(BF)
        back_send[:, side] = dot_rows(scaled, turn).astype(BF)
        for move in moves():
            s = target(move)
            pltpu.make_async_remote_copy(
                src_ref=back_send.at[pl.ds(pl.multiple_of(s * group, group), group), side],
                dst_ref=back_out.at[own_place, side],
                send_sem=back_ssem,
                recv_sem=back_rsem,
                device_id=(s, t),
                device_id_type=MESH,
            ).start()

    load_w.wait()
    cross(0)

    @pl.when(is_owner)
    def _():
        h = own
        arrive(g_full, 1)

        @pl.loop(0, 4)
        def _(step):
            jj = lax.rem(step + 2, 4)
            half = pl.ds(pl.multiple_of(jj * 256, 256), 256)
            total = jnp.dot(e_full[...], g_full[:, half], preferred_element_type=F32)
            total = total + dot_rows(g_full[...], e_full[half, :])
            lad_send[:, half] = total.astype(BF)
            for i in (3, 5, 2, 6, 1, 7, 4):
                for m in range(2):
                    j = 2 * jj + m
                    block = lad_send.at[pl.ds(i * BLK, BLK), at128(j)]
                    to = (c, lax.rem(t + i, 8))
                    nearer = (1 if i < 4 else 7, 2 if i < 4 else 6)
                    pass_on = [] if i == 4 else [4] if i in (3, 5) else [4, 3 if i < 4 else 5]
                    plain = j != i
                    for k in pass_on:
                        plain = jnp.logical_and(plain, j != k)
                    if i in (3, 5):
                        for k in nearer:
                            plain = jnp.logical_and(plain, j != k)
                    if i == 4:
                        plain = j == 0

                    @pl.when(plain)
                    def _(j=j, block=block, to=to):
                        pltpu.make_async_remote_copy(
                            src_ref=block,
                            dst_ref=lad_out.at[h, :, at128(lax.rem(t + j, 8))],
                            send_sem=lad_ssem,
                            recv_sem=lad_rsem,
                            device_id=to,
                            device_id_type=MESH,
                        ).start()

                    for n, k in enumerate(pass_on):

                        @pl.when(j == k)
                        def _(n=n, block=block, to=to):
                            pltpu.make_async_remote_copy(
                                src_ref=block,
                                dst_ref=held.at[h, n],
                                send_sem=lad_ssem,
                                recv_sem=held_rsem.at[h],
                                device_id=to,
                                device_id_type=MESH,
                            ).start()

            for m in range(2):
                j = 2 * jj + m

                @pl.when(j != 0)
                def _(j=j):
                    pltpu.make_async_copy(
                        lad_send.at[pl.ds(0, BLK), at128(j)],
                        lad_out.at[h, :, at128(lax.rem(t + j, 8))],
                        own_sem.at[0],
                    ).start()

    cross(1)

    for h in range(4):
        owner = 4 * (h % 2) + h // 2 + 2 * core
        delta = lax.rem(t - owner + 8, 8)
        far = jnp.minimum(delta, 8 - delta)
        beyond = jnp.where(delta < 4, 3, 5)

        def pass_block(n, place, h=h):
            turned[h, n] = held[h, n].T
            pltpu.make_async_copy(held.at[h, n], lad_out.at[h, :, at128(place)], pass_own).start()
            pltpu.make_async_remote_copy(
                src_ref=turned.at[h, n],
                dst_ref=lad_out.at[h, :, at128(t)],
                send_sem=pass_ssem,
                recv_sem=lad_rsem,
                device_id=(c, place),
                device_id_type=MESH,
            ).start()

        @pl.when(far == 3)
        def _(h=h, owner=owner, pass_block=pass_block):
            pltpu.make_async_copy(held.at[h, 0], held.at[h, 0], held_rsem.at[h]).wait()
            pass_block(0, lax.rem(owner + 4, 8))

        @pl.when(jnp.logical_or(far == 1, far == 2))
        def _(h=h, owner=owner, beyond=beyond, pass_block=pass_block):
            pltpu.make_async_copy(held.at[h], held.at[h], held_rsem.at[h]).wait()
            pass_block(0, lax.rem(owner + 4, 8))
            pass_block(1, lax.rem(owner + beyond, 8))

    keep = pltpu.make_async_copy(back_send.at[own_place, :], back_out.at[own_place, :], own_sem.at[1])
    keep.start()

    def drain(ref, count, sem):
        piece = ref.at[pl.ds(0, count), :]
        pltpu.make_async_copy(piece, piece, sem).wait()

    for n in range(2):
        drain(rec_e, 512 - group, a2a_send)

    @pl.when(is_owner)
    def _():
        drain(lad_send, 20 * 16, gat_send)
        drain(lad_send, 39 * 16, lad_ssem)
        drain(lad_send, 3 * 16, pass_ssem)
        drain(lad_send, 3 * 16, pass_own)
        drain(lad_send, 7 * 16, own_sem.at[0])
        drain(lad_send, 18 * 16, lad_rsem)

    @pl.when(jnp.logical_not(is_owner))
    def _():
        drain(lad_send, 36 * 16, gat_send)
        drain(lad_send, 21 * 16, lad_rsem)
        drain(lad_send, 7 * 16, pass_ssem)
        drain(lad_send, 7 * 16, pass_own)

    keep.wait()
    drain(lad_send, 4 * 16, own_sem.at[2])
    drain(rec_e, 512 - group, back_ssem)
    drain(rec_e, 512 - group, back_rsem)


def exchange(n_chan, *args):
    far = pl.BlockSpec(memory_space=pltpu.HBM)
    smem = pl.BlockSpec(memory_space=pltpu.SMEM)
    anywhere = pl.BlockSpec(memory_space=pl.ANY)
    dma = pltpu.SemaphoreType.DMA
    return pl.pallas_call(
        functools.partial(kernel, n_chan),
        name="commutator_exchange",
        out_shape=(
            jax.ShapeDtypeStruct((4, BLK, 1024), BF),
            jax.ShapeDtypeStruct((512, 1024), BF),
        ),
        in_specs=[far, far, smem, far, far, far, far],
        out_specs=(anywhere, anywhere),
        scratch_shapes=[
            pltpu.VMEM((4, BLK, 1024), BF),
            pltpu.VMEM((4, BLK, 1024), BF),
            pltpu.VMEM((512, 1024), BF),
            pltpu.VMEM((512, 1024), BF),
            pltpu.VMEM((1024, 1024), BF),
            pltpu.VMEM((1024, 1024), BF),
            pltpu.VMEM((4, BLK, BLK), BF),
            pltpu.VMEM((1024, 1024), BF),
            pltpu.VMEM((512, 1024), BF),
            pltpu.VMEM((2, 512, 512), F32),
            pltpu.VMEM((2, 512, 512), BF),
            pltpu.VMEM((512, 512), BF),
            pltpu.VMEM((512, 512), BF),
            pltpu.VMEM((4, 1, 1024), F32),
            pltpu.VMEM((2, 4, 1024), jnp.int32),
            pltpu.VMEM((2, 2, 512), jnp.int32),
            pltpu.VMEM((2, 512), jnp.int32),
            pltpu.VMEM((4, 2, BLK, BLK), BF),
            pltpu.VMEM((4, 2, BLK, BLK), BF),
            dma((5,)),
            dma,
            dma((3,)),
            dma,
            dma((2, 2)),
            dma,
            dma((2,)),
            dma,
            dma,
            dma,
            dma,
            dma((4,)),
            dma,
            dma,
        ],
        compiler_params=pltpu.CompilerParams(
            collective_id=0, has_side_effects=True, vmem_limit_bytes=VMEM_BYTES
        ),
    )(*[pltpu.with_memory_space_constraint(a, pltpu.HBM) for a in args])


def per_device(
    n_chan,
    generator,
    hamiltonian,
    chan_sizes,
    pair_occupation,
    recoupled_occupation,
    recouple_map,
    recouple_weights,
):
    chan_count, tile_rows, states = generator.shape
    ladder, back = exchange(
        n_chan,
        generator,
        hamiltonian,
        chan_sizes,
        pair_occupation,
        recoupled_occupation,
        recouple_map,
        recouple_weights,
    )
    shape = (chan_count, tile_rows, states)
    sizes = chan_sizes[:, None, None]
    row = lax.axis_index("tile") * tile_rows + lax.broadcasted_iota(jnp.int32, shape, 1)
    column = lax.broadcasted_iota(jnp.int32, shape, 2)
    total = ladder.astype(F32) + back.reshape(shape).astype(F32)
    return jnp.where((row < sizes) & (column < sizes), total, jnp.zeros((), F32)).astype(BF)


def solution(mesh):
    return jax.shard_map(
        functools.partial(per_device, mesh.shape["chan"]),
        mesh=mesh,
        in_specs=(
            P("chan", "tile", None),
            P("chan", "tile", None),
            P("chan"),
            P(None, "chan", None),
            P(None, ("chan", "tile"), None),
            P(("chan", "tile"), None),
            P(("chan", "tile"), None, None),
        ),
        out_specs=P("chan", "tile", None),
        check_vma=False,
    )
```

```python
import functools

import jax
import jax.numpy as jnp
from jax import lax
from jax.experimental import pallas as pl
from jax.experimental.pallas import tpu as pltpu
from jax.sharding import PartitionSpec as P

MESH = pl.DeviceIdType.MESH
BF = jnp.bfloat16
F32 = jnp.float32
BLK = 128
VMEM_BYTES = 30 * 1024 * 1024

ORDER = (0, 1, 7, 2, 6, 3, 5, 4)


def pairs_of(flip_ties):
    found = []
    for i in range(8):
        for j in range(i + 1, 8):
            a, b = ORDER[i], ORDER[j]
            if flip_ties and a + b == 8:
                a, b = b, a
            found.append((a, b))
    return found


def hops(move):
    return min(move[0], 4 - move[0]) + min(move[1], 4 - move[1])


def moves():
    listed = []
    everything = [(x, y, k) for y in range(4) for x in range(4) for k in range(2) if (x, y, k) != (0, 0, 0)]
    for far in (1, 2, 3, 4, 0):
        left = [m for m in everything if hops(m) == far]
        taken = []
        while left:
            recent = taken[-3:][::-1]
            cost = lambda m: sum(((m[0] == p[0]) + (m[1] == p[1])) * (3 - i) for i, p in enumerate(recent))
            taken.append(min(left, key=cost))
            left.remove(taken[-1])
        listed += taken
    return listed[::-1]


def passed(i):
    return {0: (), 4: (), 3: (4,), 5: (4,)}.get(i, (4, 3 if i < 4 else 5))


def dot_rows(a, b):
    return lax.dot_general(a, b, (((1,), (1,)), ((), ())), preferred_element_type=F32)


def at128(index):
    return pl.ds(pl.multiple_of(index * BLK, BLK), BLK)


def kernel(
    n_chan,
    e_hbm,
    g_hbm,
    sizes,
    pocc_hbm,
    rocc_hbm,
    cmap_hbm,
    w_hbm,
    lad_out,
    back_out,
    e_m,
    g_m,
    rec_e,
    rec_g,
    e_full,
    g_full,
    diag,
    lad_send,
    back_send,
    wts,
    onehot,
    e_bar,
    g_bar,
    wrow,
    pocc,
    rocc,
    cmap,
    held,
    turned,
    load_sem,
    w_sem,
    own_sem,
    a2a_send,
    a2a_recv,
    gat_send,
    gat_recv,
    lad_ssem,
    lad_rsem,
    back_ssem,
    back_rsem,
    held_rsem,
    pass_ssem,
    pass_own,
):
    c = lax.axis_index("chan")
    t = lax.axis_index("tile")
    core = lax.rem(c, 2)
    group = 512 // n_chan

    def target(move):
        x, y, k = move
        return lax.rem(c // 8 + y, 4) * 8 + lax.rem(c // 2 + x, 4) * 2 + lax.rem(core + k, 2)

    load_e = pltpu.make_async_copy(e_hbm, e_m, load_sem.at[0])
    load_g = pltpu.make_async_copy(g_hbm, g_m, load_sem.at[1])
    load_e.start()
    load_g.start()
    small = [
        pltpu.make_async_copy(src, dst, load_sem.at[n])
        for n, (src, dst) in enumerate(((pocc_hbm, pocc), (cmap_hbm, cmap), (rocc_hbm, rocc)), 2)
    ]
    for load in small:
        load.start()
    load_w = pltpu.make_async_copy(w_hbm, wts, w_sem)
    load_w.start()

    barrier = pltpu.get_barrier_semaphore()

    @pl.loop(1, n_chan)
    def _(k):
        pl.semaphore_signal(barrier, inc=1, device_id=(c ^ k, t), device_id_type=MESH)

    @pl.loop(1, 8)
    def _(k):
        pl.semaphore_signal(barrier, inc=1, device_id=(c, lax.rem(t + k, 8)), device_id_type=MESH)

    cols = lax.broadcasted_iota(jnp.int32, (1, 1024), 1)
    rows = lax.broadcasted_iota(jnp.int32, (BLK, 1), 0) + t * BLK
    load_e.wait()
    load_g.wait()
    small[0].wait()
    for h in range(4):
        size = sizes[h]
        col_live = (cols < size).astype(F32)
        row_live = (rows < size).astype(F32)
        wrow[h] = (1 - pocc[0, pl.ds(h, 1), :] - pocc[1, pl.ds(h, 1), :]).astype(F32) * col_live
        live = (row_live * col_live).astype(BF)
        e_m[h] = e_m[h] * live
        g_m[h] = g_m[h] * live

    pl.semaphore_wait(barrier, n_chan + 6)

    def gather(src, dst, which, phase):
        for h in (2 * phase, 2 * phase + 1):
            owner = 4 * (h % 2) + phase + 2 * core
            delta = lax.rem(t - owner + 8, 8)
            far = jnp.minimum(delta, 8 - delta)

            def send(j, h=h, owner=owner, delta=delta):
                pltpu.make_async_remote_copy(
                    src_ref=src.at[h, :, at128(lax.rem(owner + j, 8))],
                    dst_ref=dst.at[at128(delta), at128(j)],
                    send_sem=gat_send,
                    recv_sem=gat_recv.at[which],
                    device_id=(c, owner),
                    device_id_type=MESH,
                ).start()

            @pl.when(delta != 0)
            def _(send=send, far=far, delta=delta):
                send(delta)

                @pl.when(delta > 4 if which else delta < 4)
                def _():
                    send(8 - delta)

                @pl.loop(far + 1, 8 - far)
                def _(j):
                    send(j)

    gather(e_m, e_full, 0, 0)
    gather(g_m, g_full, 1, 0)
    gather(e_m, e_full, 0, 1)
    gather(g_m, g_full, 1, 1)

    own_place = pl.ds(pl.multiple_of(c * group, group), group)

    @pl.loop(0, 2)
    def _(q):
        side = pl.ds(pl.multiple_of(q * 512, 512), 512)
        for move in moves():
            s = target(move)
            first = pl.multiple_of(lax.rem(s * group, BLK), group)
            for n, (src, dst) in enumerate(((e_m, rec_e), (g_m, rec_g))):
                pltpu.make_async_remote_copy(
                    src_ref=src.at[(s * group) // BLK, pl.ds(first, group), side],
                    dst_ref=dst.at[own_place, side],
                    send_sem=a2a_send,
                    recv_sem=a2a_recv.at[q, n],
                    device_id=(s, t),
                    device_id_type=MESH,
                ).start()


    own_h = (c * group) // BLK
    own_rows = pl.ds(pl.multiple_of(lax.rem(c * group, BLK), group), group)
    rec_e[own_place, :] = e_m[own_h, own_rows, :]
    rec_g[own_place, :] = g_m[own_h, own_rows, :]

    small[1].wait()
    small[2].wait()
    for q in range(2):
        spots = lax.broadcasted_iota(jnp.int32, (512, 512), 0)
        onehot[q] = (spots == cmap[pl.ds(q, 1), :]).astype(F32).astype(BF)

    for h in range(4):
        weight = wrow[h].astype(BF)
        mine = dot_rows(e_m[h] * weight, g_m[h]) + dot_rows(g_m[h] * weight, e_m[h])
        diag[h] = mine.astype(BF)
        pltpu.make_async_copy(diag.at[h], lad_out.at[h, :, at128(t)], own_sem.at[2]).start()

    is_owner = lax.rem(t // 2, 2) == core
    own = 2 * lax.rem(t, 2) + t // 4

    def arrive(full, which):
        landed = full.at[pl.ds(0, 28 * 16), :]
        pltpu.make_async_copy(landed, landed, gat_recv.at[which]).wait()
        for a, b in pairs_of(which):
            block = full[pl.ds(a * BLK, BLK), pl.ds(b * BLK, BLK)].T
            full[pl.ds(b * BLK, BLK), pl.ds(a * BLK, BLK)] = block if which else -block

    @pl.when(is_owner)
    def _():
        for j in range(8):
            place = at128(lax.rem(t + j, 8))
            here = pl.ds(j * BLK, BLK)
            e_full[pl.ds(0, BLK), here] = e_m[own, :, place]
            g_full[pl.ds(0, BLK), here] = g_m[own, :, place]
        arrive(e_full, 0)
        for j in range(8):
            here = pl.ds(j * BLK, BLK)
            weight = wrow[own, :, at128(lax.rem(t + j, 8))].astype(BF)
            e_full[:, here] = e_full[:, here] * weight

    def cross(q):
        side = pl.ds(q * 512, 512)
        for n, rec in enumerate((rec_e, rec_g)):
            landed = rec.at[pl.ds(0, 512 - group), side]
            pltpu.make_async_copy(landed, landed, a2a_recv.at[q, n]).wait()
        turn = onehot[q]
        scale = wts[q]
        e_bar[...] = (jnp.dot(rec_e[:, side], turn, preferred_element_type=F32) * scale).astype(BF)
        g_bar[...] = (jnp.dot(rec_g[:, side], turn, preferred_element_type=F32) * scale).astype(BF)
        signs = (rocc[0, pl.ds(q, 1), :] - rocc[1, pl.ds(q, 1), :]).astype(F32).astype(BF)
        crossed = jnp.dot(e_bar[...] * signs, g_bar[...], preferred_element_type=F32)
        crossed = crossed - jnp.dot(g_bar[...] * signs, e_bar[...], preferred_element_type=F32)
        scaled = (crossed * scale).astype(BF)
        back_send[:, side] = dot_rows(scaled, turn).astype(BF)
        for move in moves():
            s = target(move)
            pltpu.make_async_remote_copy(
                src_ref=back_send.at[pl.ds(pl.multiple_of(s * group, group), group), side],
                dst_ref=back_out.at[own_place, side],
                send_sem=back_ssem,
                recv_sem=back_rsem,
                device_id=(s, t),
                device_id_type=MESH,
            ).start()

    def ladder():
        h = own
        arrive(g_full, 1)

        @pl.loop(0, 4)
        def _(step):
            jj = lax.rem(6 - step, 4)
            half = pl.ds(pl.multiple_of(jj * 256, 256), 256)
            total = jnp.dot(e_full[...], g_full[:, half], preferred_element_type=F32)
            total = total + dot_rows(g_full[...], e_full[half, :])
            lad_send[:, half] = total.astype(BF)

            def give(i, j, dst, sem):
                pltpu.make_async_remote_copy(
                    src_ref=lad_send.at[pl.ds(i * BLK, BLK), at128(j)],
                    dst_ref=dst,
                    send_sem=lad_ssem,
                    recv_sem=sem,
                    device_id=(c, lax.rem(t + i, 8)),
                    device_id_type=MESH,
                ).start()

            for i in (1, 7, 2, 6, 3, 5):
                for m in range(2):
                    j = 2 * jj + m
                    for n, k in enumerate(passed(i)):

                        @pl.when(j == k)
                        def _(i=i, j=j, n=n):
                            give(i, j, held.at[h, n], held_rsem.at[h])

            for i in (3, 5, 2, 6, 1, 7, 4):
                for m in range(2):
                    j = 2 * jj + m
                    plain = j == 0
                    if i != 4:
                        plain = j != i
                        for k in passed(i) + ((1, 2) if i == 3 else (6, 7) if i == 5 else ()):
                            plain = jnp.logical_and(plain, j != k)

                    @pl.when(plain)
                    def _(i=i, j=j):
                        give(i, j, lad_out.at[h, :, at128(lax.rem(t + j, 8))], lad_rsem)

            for m in range(2):
                j = 2 * jj + m

                @pl.when(j != 0)
                def _(j=j):
                    pltpu.make_async_copy(
                        lad_send.at[pl.ds(0, BLK), at128(j)],
                        lad_out.at[h, :, at128(lax.rem(t + j, 8))],
                        own_sem.at[0],
                    ).start()

    late = lax.rem(t, 2) == 1

    @pl.when(jnp.logical_and(is_owner, jnp.logical_not(late)))
    def _():
        ladder()

    load_w.wait()
    cross(0)

    @pl.when(jnp.logical_and(is_owner, late))
    def _():
        ladder()

    cross(1)

    for h in range(4):
        owner = 4 * (h % 2) + h // 2 + 2 * core
        delta = lax.rem(t - owner + 8, 8)
        far = jnp.minimum(delta, 8 - delta)
        beyond = jnp.where(delta < 4, 3, 5)

        def pass_block(n, place, h=h):
            turned[h, n] = held[h, n].T
            pltpu.make_async_copy(held.at[h, n], lad_out.at[h, :, at128(place)], pass_own).start()
            pltpu.make_async_remote_copy(
                src_ref=turned.at[h, n],
                dst_ref=lad_out.at[h, :, at128(t)],
                send_sem=pass_ssem,
                recv_sem=lad_rsem,
                device_id=(c, place),
                device_id_type=MESH,
            ).start()

        @pl.when(far == 3)
        def _(h=h, owner=owner, pass_block=pass_block):
            pltpu.make_async_copy(held.at[h, 0], held.at[h, 0], held_rsem.at[h]).wait()
            pass_block(0, lax.rem(owner + 4, 8))

        @pl.when(jnp.logical_or(far == 1, far == 2))
        def _(h=h, owner=owner, beyond=beyond, pass_block=pass_block):
            pltpu.make_async_copy(held.at[h], held.at[h], held_rsem.at[h]).wait()
            pass_block(0, lax.rem(owner + 4, 8))
            pass_block(1, lax.rem(owner + beyond, 8))

    keep = pltpu.make_async_copy(back_send.at[own_place, :], back_out.at[own_place, :], own_sem.at[1])
    keep.start()

    def drain(ref, count, sem):
        piece = ref.at[pl.ds(0, count), :]
        pltpu.make_async_copy(piece, piece, sem).wait()

    for n in range(2):
        drain(rec_e, 512 - group, a2a_send)

    @pl.when(is_owner)
    def _():
        drain(lad_send, 20 * 16, gat_send)
        drain(lad_send, 39 * 16, lad_ssem)
        drain(lad_send, 3 * 16, pass_ssem)
        drain(lad_send, 3 * 16, pass_own)
        drain(lad_send, 7 * 16, own_sem.at[0])
        drain(lad_send, 18 * 16, lad_rsem)

    @pl.when(jnp.logical_not(is_owner))
    def _():
        drain(lad_send, 36 * 16, gat_send)
        drain(lad_send, 21 * 16, lad_rsem)
        drain(lad_send, 7 * 16, pass_ssem)
        drain(lad_send, 7 * 16, pass_own)

    keep.wait()
    drain(lad_send, 4 * 16, own_sem.at[2])
    drain(rec_e, 512 - group, back_ssem)
    drain(rec_e, 512 - group, back_rsem)


def exchange(n_chan, *args):
    far = pl.BlockSpec(memory_space=pltpu.HBM)
    smem = pl.BlockSpec(memory_space=pltpu.SMEM)
    anywhere = pl.BlockSpec(memory_space=pl.ANY)
    dma = pltpu.SemaphoreType.DMA
    return pl.pallas_call(
        functools.partial(kernel, n_chan),
        name="commutator_exchange",
        out_shape=(
            jax.ShapeDtypeStruct((4, BLK, 1024), BF),
            jax.ShapeDtypeStruct((512, 1024), BF),
        ),
        in_specs=[far, far, smem, far, far, far, far],
        out_specs=(anywhere, anywhere),
        scratch_shapes=[
            pltpu.VMEM((4, BLK, 1024), BF),
            pltpu.VMEM((4, BLK, 1024), BF),
            pltpu.VMEM((512, 1024), BF),
            pltpu.VMEM((512, 1024), BF),
            pltpu.VMEM((1024, 1024), BF),
            pltpu.VMEM((1024, 1024), BF),
            pltpu.VMEM((4, BLK, BLK), BF),
            pltpu.VMEM((1024, 1024), BF),
            pltpu.VMEM((512, 1024), BF),
            pltpu.VMEM((2, 512, 512), F32),
            pltpu.VMEM((2, 512, 512), BF),
            pltpu.VMEM((512, 512), BF),
            pltpu.VMEM((512, 512), BF),
            pltpu.VMEM((4, 1, 1024), F32),
            pltpu.VMEM((2, 4, 1024), jnp.int32),
            pltpu.VMEM((2, 2, 512), jnp.int32),
            pltpu.VMEM((2, 512), jnp.int32),
            pltpu.VMEM((4, 2, BLK, BLK), BF),
            pltpu.VMEM((4, 2, BLK, BLK), BF),
            dma((5,)),
            dma,
            dma((3,)),
            dma,
            dma((2, 2)),
            dma,
            dma((2,)),
            dma,
            dma,
            dma,
            dma,
            dma((4,)),
            dma,
            dma,
        ],
        compiler_params=pltpu.CompilerParams(
            collective_id=0, has_side_effects=True, vmem_limit_bytes=VMEM_BYTES
        ),
    )(*[pltpu.with_memory_space_constraint(a, pltpu.HBM) for a in args])


def per_device(
    n_chan,
    generator,
    hamiltonian,
    chan_sizes,
    pair_occupation,
    recoupled_occupation,
    recouple_map,
    recouple_weights,
):
    chan_count, tile_rows, states = generator.shape
    ladder, back = exchange(
        n_chan,
        generator,
        hamiltonian,
        chan_sizes,
        pair_occupation,
        recoupled_occupation,
        recouple_map,
        recouple_weights,
    )
    shape = (chan_count, tile_rows, states)
    sizes = chan_sizes[:, None, None]
    row = lax.axis_index("tile") * tile_rows + lax.broadcasted_iota(jnp.int32, shape, 1)
    column = lax.broadcasted_iota(jnp.int32, shape, 2)
    total = ladder.astype(F32) + back.reshape(shape).astype(F32)
    return jnp.where((row < sizes) & (column < sizes), total, jnp.zeros((), F32)).astype(BF)


def solution(mesh):
    return jax.shard_map(
        functools.partial(per_device, mesh.shape["chan"]),
        mesh=mesh,
        in_specs=(
            P("chan", "tile", None),
            P("chan", "tile", None),
            P("chan"),
            P(None, "chan", None),
            P(None, ("chan", "tile"), None),
            P(("chan", "tile"), None),
            P(("chan", "tile"), None, None),
        ),
        out_specs=P("chan", "tile", None),
        check_vma=False,
    )
```

```python
import functools

import jax
import jax.numpy as jnp
from jax import lax
from jax.experimental import pallas as pl
from jax.experimental.pallas import tpu as pltpu
from jax.sharding import PartitionSpec as P

MESH = pl.DeviceIdType.MESH
BF = jnp.bfloat16
F32 = jnp.float32
BLK = 128
VMEM_BYTES = 30 * 1024 * 1024

ORDER = (0, 1, 7, 2, 6, 3, 5, 4)


def pairs_of(flip_ties):
    found = []
    for i in range(8):
        for j in range(i + 1, 8):
            a, b = ORDER[i], ORDER[j]
            if flip_ties and a + b == 8:
                a, b = b, a
            found.append((a, b))
    return found


def hops(move):
    return min(move[0], 4 - move[0]) + min(move[1], 4 - move[1])


def moves():
    listed = []
    everything = [(x, y, k) for y in range(4) for x in range(4) for k in range(2) if (x, y, k) != (0, 0, 0)]
    for far in (1, 2, 3, 4, 0):
        left = [m for m in everything if hops(m) == far]
        taken = []
        while left:
            recent = taken[-3:][::-1]
            cost = lambda m: sum(((m[0] == p[0]) + (m[1] == p[1])) * (3 - i) for i, p in enumerate(recent))
            taken.append(min(left, key=cost))
            left.remove(taken[-1])
        listed += taken
    return listed[::-1]


def passed(i):
    return {0: (), 4: (), 3: (4,), 5: (4,)}.get(i, (4, 3 if i < 4 else 5))


def dot_rows(a, b):
    return lax.dot_general(a, b, (((1,), (1,)), ((), ())), preferred_element_type=F32)


def at128(index):
    return pl.ds(pl.multiple_of(index * BLK, BLK), BLK)


def kernel(
    n_chan,
    e_hbm,
    g_hbm,
    sizes,
    pocc_hbm,
    rocc_hbm,
    cmap_hbm,
    w_hbm,
    out,
    lad_out,
    back_out,
    e_m,
    g_m,
    rec_e,
    rec_g,
    e_full,
    g_full,
    diag,
    lad_send,
    back_send,
    wts,
    onehot,
    e_bar,
    g_bar,
    wrow,
    pocc,
    rocc,
    cmap,
    held,
    turned,
    load_sem,
    w_sem,
    own_sem,
    a2a_send,
    a2a_recv,
    gat_send,
    gat_recv,
    lad_ssem,
    lad_rsem,
    back_ssem,
    back_rsem,
    held_rsem,
    pass_ssem,
    pass_own,
):
    c = lax.axis_index("chan")
    t = lax.axis_index("tile")
    core = lax.rem(c, 2)
    group = 512 // n_chan

    def target(move):
        x, y, k = move
        return lax.rem(c // 8 + y, 4) * 8 + lax.rem(c // 2 + x, 4) * 2 + lax.rem(core + k, 2)

    load_e = pltpu.make_async_copy(e_hbm, e_m, load_sem.at[0])
    load_g = pltpu.make_async_copy(g_hbm, g_m, load_sem.at[1])
    load_e.start()
    load_g.start()
    small = [
        pltpu.make_async_copy(src, dst, load_sem.at[n])
        for n, (src, dst) in enumerate(((pocc_hbm, pocc), (cmap_hbm, cmap), (rocc_hbm, rocc)), 2)
    ]
    for load in small:
        load.start()
    load_w = pltpu.make_async_copy(w_hbm, wts, w_sem)

    barrier = pltpu.get_barrier_semaphore()

    @pl.loop(1, n_chan)
    def _(k):
        pl.semaphore_signal(barrier, inc=1, device_id=(c ^ k, t), device_id_type=MESH)

    @pl.loop(1, 8)
    def _(k):
        pl.semaphore_signal(barrier, inc=1, device_id=(c, lax.rem(t + k, 8)), device_id_type=MESH)

    cols = lax.broadcasted_iota(jnp.int32, (1, 1024), 1)
    rows = lax.broadcasted_iota(jnp.int32, (BLK, 1), 0) + t * BLK
    load_e.wait()
    load_g.wait()
    small[0].wait()
    for h in range(4):
        size = sizes[h]
        col_live = (cols < size).astype(F32)
        row_live = (rows < size).astype(F32)
        wrow[h] = (1 - pocc[0, pl.ds(h, 1), :] - pocc[1, pl.ds(h, 1), :]).astype(F32) * col_live
        live = (row_live * col_live).astype(BF)
        e_m[h] = e_m[h] * live
        g_m[h] = g_m[h] * live

    load_w.start()
    pl.semaphore_wait(barrier, n_chan + 6)

    def gather(src, dst, which, phase):
        for h in (2 * phase, 2 * phase + 1):
            owner = 4 * (h % 2) + phase + 2 * core
            delta = lax.rem(t - owner + 8, 8)
            far = jnp.minimum(delta, 8 - delta)

            def send(j, h=h, owner=owner, delta=delta):
                pltpu.make_async_remote_copy(
                    src_ref=src.at[h, :, at128(lax.rem(owner + j, 8))],
                    dst_ref=dst.at[at128(delta), at128(j)],
                    send_sem=gat_send,
                    recv_sem=gat_recv.at[which],
                    device_id=(c, owner),
                    device_id_type=MESH,
                ).start()

            @pl.when(delta != 0)
            def _(send=send, far=far, delta=delta):
                send(delta)

                @pl.when(delta > 4 if which else delta < 4)
                def _():
                    send(8 - delta)

                @pl.loop(far + 1, 8 - far)
                def _(j):
                    send(j)

    gather(e_m, e_full, 0, 0)
    gather(g_m, g_full, 1, 0)
    gather(e_m, e_full, 0, 1)
    gather(g_m, g_full, 1, 1)

    own_place = pl.ds(pl.multiple_of(c * group, group), group)

    @pl.loop(0, 2)
    def _(q):
        side = pl.ds(pl.multiple_of(q * 512, 512), 512)
        for move in moves():
            s = target(move)
            first = pl.multiple_of(lax.rem(s * group, BLK), group)
            for n, (src, dst) in enumerate(((e_m, rec_e), (g_m, rec_g))):
                pltpu.make_async_remote_copy(
                    src_ref=src.at[(s * group) // BLK, pl.ds(first, group), side],
                    dst_ref=dst.at[own_place, side],
                    send_sem=a2a_send,
                    recv_sem=a2a_recv.at[q, n],
                    device_id=(s, t),
                    device_id_type=MESH,
                ).start()


    own_h = (c * group) // BLK
    own_rows = pl.ds(pl.multiple_of(lax.rem(c * group, BLK), group), group)
    rec_e[own_place, :] = e_m[own_h, own_rows, :]
    rec_g[own_place, :] = g_m[own_h, own_rows, :]

    small[1].wait()
    small[2].wait()
    for q in range(2):
        spots = lax.broadcasted_iota(jnp.int32, (512, 512), 0)
        onehot[q] = (spots == cmap[pl.ds(q, 1), :]).astype(F32).astype(BF)

    for h in range(4):
        weight = wrow[h].astype(BF)
        mine = dot_rows(e_m[h] * weight, g_m[h]) + dot_rows(g_m[h] * weight, e_m[h])
        diag[h] = mine.astype(BF)
        pltpu.make_async_copy(diag.at[h], lad_out.at[h, :, at128(t)], own_sem.at[2]).start()

    is_owner = lax.rem(t // 2, 2) == core
    own = 2 * lax.rem(t, 2) + t // 4

    def arrive(full, which):
        landed = full.at[pl.ds(0, 28 * 16), :]
        pltpu.make_async_copy(landed, landed, gat_recv.at[which]).wait()
        for a, b in pairs_of(which):
            block = full[pl.ds(a * BLK, BLK), pl.ds(b * BLK, BLK)].T
            full[pl.ds(b * BLK, BLK), pl.ds(a * BLK, BLK)] = block if which else -block

    @pl.when(is_owner)
    def _():
        for j in range(8):
            place = at128(lax.rem(t + j, 8))
            here = pl.ds(j * BLK, BLK)
            e_full[pl.ds(0, BLK), here] = e_m[own, :, place]
            g_full[pl.ds(0, BLK), here] = g_m[own, :, place]
        arrive(e_full, 0)
        for j in range(8):
            here = pl.ds(j * BLK, BLK)
            weight = wrow[own, :, at128(lax.rem(t + j, 8))].astype(BF)
            e_full[:, here] = e_full[:, here] * weight

    def cross(q):
        side = pl.ds(q * 512, 512)
        for n, rec in enumerate((rec_e, rec_g)):
            landed = rec.at[pl.ds(0, 512 - group), side]
            pltpu.make_async_copy(landed, landed, a2a_recv.at[q, n]).wait()
        turn = onehot[q]
        scale = wts[q]
        e_bar[...] = (jnp.dot(rec_e[:, side], turn, preferred_element_type=F32) * scale).astype(BF)
        g_bar[...] = (jnp.dot(rec_g[:, side], turn, preferred_element_type=F32) * scale).astype(BF)
        signs = (rocc[0, pl.ds(q, 1), :] - rocc[1, pl.ds(q, 1), :]).astype(F32).astype(BF)
        crossed = jnp.dot(e_bar[...] * signs, g_bar[...], preferred_element_type=F32)
        crossed = crossed - jnp.dot(g_bar[...] * signs, e_bar[...], preferred_element_type=F32)
        scaled = (crossed * scale).astype(BF)
        back_send[:, side] = dot_rows(scaled, turn).astype(BF)
        for move in moves():
            s = target(move)
            pltpu.make_async_remote_copy(
                src_ref=back_send.at[pl.ds(pl.multiple_of(s * group, group), group), side],
                dst_ref=back_out.at[own_place, side],
                send_sem=back_ssem,
                recv_sem=back_rsem,
                device_id=(s, t),
                device_id_type=MESH,
            ).start()

    def ladder():
        h = own
        arrive(g_full, 1)

        @pl.loop(0, 4)
        def _(step):
            jj = lax.rem(6 - step, 4)
            half = pl.ds(pl.multiple_of(jj * 256, 256), 256)
            total = jnp.dot(e_full[...], g_full[:, half], preferred_element_type=F32)
            total = total + dot_rows(g_full[...], e_full[half, :])
            lad_send[:, half] = total.astype(BF)

            def give(i, j, dst, sem):
                pltpu.make_async_remote_copy(
                    src_ref=lad_send.at[pl.ds(i * BLK, BLK), at128(j)],
                    dst_ref=dst,
                    send_sem=lad_ssem,
                    recv_sem=sem,
                    device_id=(c, lax.rem(t + i, 8)),
                    device_id_type=MESH,
                ).start()

            for i in (1, 7, 2, 6, 3, 5):
                for m in range(2):
                    j = 2 * jj + m
                    for n, k in enumerate(passed(i)):

                        @pl.when(j == k)
                        def _(i=i, j=j, n=n):
                            give(i, j, held.at[h, n], held_rsem.at[h])

            for i in (3, 5, 2, 6, 1, 7, 4):
                for m in range(2):
                    j = 2 * jj + m
                    plain = j == 0
                    if i != 4:
                        plain = j != i
                        for k in passed(i) + ((1, 2) if i == 3 else (6, 7) if i == 5 else ()):
                            plain = jnp.logical_and(plain, j != k)

                    @pl.when(plain)
                    def _(i=i, j=j):
                        give(i, j, lad_out.at[h, :, at128(lax.rem(t + j, 8))], lad_rsem.at[h])

            for m in range(2):
                j = 2 * jj + m

                @pl.when(j != 0)
                def _(j=j):
                    pltpu.make_async_copy(
                        lad_send.at[pl.ds(0, BLK), at128(j)],
                        lad_out.at[h, :, at128(lax.rem(t + j, 8))],
                        own_sem.at[0],
                    ).start()

    def pass_on(h):
        owner = 4 * (h % 2) + h // 2 + 2 * core
        delta = lax.rem(t - owner + 8, 8)
        far = jnp.minimum(delta, 8 - delta)
        beyond = jnp.where(delta < 4, 3, 5)

        def pass_block(n, place, h=h):
            turned[h, n] = held[h, n].T
            pltpu.make_async_copy(held.at[h, n], lad_out.at[h, :, at128(place)], pass_own).start()
            pltpu.make_async_remote_copy(
                src_ref=turned.at[h, n],
                dst_ref=lad_out.at[h, :, at128(t)],
                send_sem=pass_ssem,
                recv_sem=lad_rsem.at[h],
                device_id=(c, place),
                device_id_type=MESH,
            ).start()

        @pl.when(far == 3)
        def _(h=h, owner=owner, pass_block=pass_block):
            pltpu.make_async_copy(held.at[h, 0], held.at[h, 0], held_rsem.at[h]).wait()
            pass_block(0, lax.rem(owner + 4, 8))

        @pl.when(jnp.logical_or(far == 1, far == 2))
        def _(h=h, owner=owner, beyond=beyond, pass_block=pass_block):
            pltpu.make_async_copy(held.at[h], held.at[h], held_rsem.at[h]).wait()
            pass_block(0, lax.rem(owner + 4, 8))
            pass_block(1, lax.rem(owner + beyond, 8))

    late = lax.rem(t, 2) == 1

    @pl.when(jnp.logical_and(is_owner, jnp.logical_not(late)))
    def _():
        ladder()

    load_w.wait()
    cross(0)

    @pl.when(jnp.logical_and(is_owner, late))
    def _():
        ladder()

    pass_on(0)
    pass_on(1)
    cross(1)
    pass_on(2)
    pass_on(3)

    keep = pltpu.make_async_copy(back_send.at[own_place, :], back_out.at[own_place, :], own_sem.at[1])
    keep.start()

    def drain(ref, count, sem):
        piece = ref.at[pl.ds(0, count), :]
        pltpu.make_async_copy(piece, piece, sem).wait()

    for n in range(2):
        drain(rec_e, 512 - group, a2a_send)

    @pl.when(is_owner)
    def _():
        drain(lad_send, 20 * 16, gat_send)
        drain(lad_send, 39 * 16, lad_ssem)
        drain(lad_send, 3 * 16, pass_ssem)
        drain(lad_send, 3 * 16, pass_own)
        drain(lad_send, 7 * 16, own_sem.at[0])

    @pl.when(jnp.logical_not(is_owner))
    def _():
        drain(lad_send, 36 * 16, gat_send)
        drain(lad_send, 7 * 16, pass_ssem)
        drain(lad_send, 7 * 16, pass_own)

    keep.wait()
    drain(lad_send, 4 * 16, own_sem.at[2])
    drain(rec_e, 512 - group, back_ssem)
    drain(rec_e, 512 - group, back_rsem)

    for h in range(4):
        delta = lax.rem(t - (4 * (h % 2) + h // 2 + 2 * core) + 8, 8)
        far = jnp.minimum(delta, 8 - delta)

        @pl.when(jnp.logical_or(far == 1, far == 2))
        def _(h=h):
            drain(lad_send, 5 * 16, lad_rsem.at[h])

        @pl.when(far == 3)
        def _(h=h):
            drain(lad_send, 6 * 16, lad_rsem.at[h])

        @pl.when(far == 4)
        def _(h=h):
            drain(lad_send, 7 * 16, lad_rsem.at[h])

        size = sizes[h]
        live = (rows < size).astype(F32) * (cols < size).astype(F32)
        total = lad_out[h].astype(F32) + back_out[pl.ds(h * BLK, BLK), :].astype(F32)
        out[h] = jnp.where(live > 0, total, 0.0).astype(BF)


def exchange(n_chan, *args):
    far = pl.BlockSpec(memory_space=pltpu.HBM)
    smem = pl.BlockSpec(memory_space=pltpu.SMEM)
    dma = pltpu.SemaphoreType.DMA
    return pl.pallas_call(
        functools.partial(kernel, n_chan),
        name="commutator_exchange",
        out_shape=jax.ShapeDtypeStruct((4, BLK, 1024), BF),
        in_specs=[far, far, smem, far, far, far, far],
        out_specs=pl.BlockSpec(memory_space=pltpu.VMEM),
        scratch_shapes=[
            pltpu.VMEM((4, BLK, 1024), BF),
            pltpu.VMEM((512, 1024), BF),
            pltpu.VMEM((4, BLK, 1024), BF),
            pltpu.VMEM((4, BLK, 1024), BF),
            pltpu.VMEM((512, 1024), BF),
            pltpu.VMEM((512, 1024), BF),
            pltpu.VMEM((1024, 1024), BF),
            pltpu.VMEM((1024, 1024), BF),
            pltpu.VMEM((4, BLK, BLK), BF),
            pltpu.VMEM((1024, 1024), BF),
            pltpu.VMEM((512, 1024), BF),
            pltpu.VMEM((2, 512, 512), F32),
            pltpu.VMEM((2, 512, 512), BF),
            pltpu.VMEM((512, 512), BF),
            pltpu.VMEM((512, 512), BF),
            pltpu.VMEM((4, 1, 1024), F32),
            pltpu.VMEM((2, 4, 1024), jnp.int32),
            pltpu.VMEM((2, 2, 512), jnp.int32),
            pltpu.VMEM((2, 512), jnp.int32),
            pltpu.VMEM((4, 2, BLK, BLK), BF),
            pltpu.VMEM((4, 2, BLK, BLK), BF),
            dma((5,)),
            dma,
            dma((3,)),
            dma,
            dma((2, 2)),
            dma,
            dma((2,)),
            dma,
            dma((4,)),
            dma,
            dma,
            dma((4,)),
            dma,
            dma,
        ],
        compiler_params=pltpu.CompilerParams(
            collective_id=0, has_side_effects=True, vmem_limit_bytes=VMEM_BYTES
        ),
    )(*[pltpu.with_memory_space_constraint(a, pltpu.HBM) for a in args])


def per_device(
    n_chan,
    generator,
    hamiltonian,
    chan_sizes,
    pair_occupation,
    recoupled_occupation,
    recouple_map,
    recouple_weights,
):
    return exchange(
        n_chan,
        generator,
        hamiltonian,
        chan_sizes,
        pair_occupation,
        recoupled_occupation,
        recouple_map,
        recouple_weights,
    )


def solution(mesh):
    return jax.shard_map(
        functools.partial(per_device, mesh.shape["chan"]),
        mesh=mesh,
        in_specs=(
            P("chan", "tile", None),
            P("chan", "tile", None),
            P("chan"),
            P(None, "chan", None),
            P(None, ("chan", "tile"), None),
            P(("chan", "tile"), None),
            P(("chan", "tile"), None, None),
        ),
        out_specs=P("chan", "tile", None),
        check_vma=False,
    )
```

```python
import functools

import jax
import jax.numpy as jnp
from jax import lax
from jax.experimental import pallas as pl
from jax.experimental.pallas import tpu as pltpu
from jax.sharding import PartitionSpec as P

MESH = pl.DeviceIdType.MESH
BF = jnp.bfloat16
F32 = jnp.float32
BLK = 128
VMEM_BYTES = 30 * 1024 * 1024

ORDER = (0, 1, 7, 2, 6, 3, 5, 4)


def pairs_of(flip_ties):
    found = []
    for i in range(8):
        for j in range(i + 1, 8):
            a, b = ORDER[i], ORDER[j]
            if flip_ties and a + b == 8:
                a, b = b, a
            found.append((a, b))
    return found


def hops(move):
    return min(move[0], 4 - move[0]) + min(move[1], 4 - move[1])


def moves():
    listed = []
    everything = [(x, y, k) for y in range(4) for x in range(4) for k in range(2) if (x, y, k) != (0, 0, 0)]
    for far in (1, 2, 3, 4, 0):
        left = [m for m in everything if hops(m) == far]
        taken = []
        while left:
            recent = taken[-3:][::-1]
            cost = lambda m: sum(((m[0] == p[0]) + (m[1] == p[1])) * (3 - i) for i, p in enumerate(recent))
            taken.append(min(left, key=cost))
            left.remove(taken[-1])
        listed += taken
    return listed[::-1]


def passed(i):
    return {0: (), 4: (), 3: (4,), 5: (4,)}.get(i, (4, 3 if i < 4 else 5))


def dot_rows(a, b):
    return lax.dot_general(a, b, (((1,), (1,)), ((), ())), preferred_element_type=F32)


def at128(index):
    return pl.ds(pl.multiple_of(index * BLK, BLK), BLK)


def kernel(
    n_chan,
    e_hbm,
    g_hbm,
    sizes,
    pocc_hbm,
    rocc_hbm,
    cmap_hbm,
    w_hbm,
    out,
    lad_out,
    back_out,
    e_m,
    g_m,
    rec_e,
    rec_g,
    e_full,
    g_full,
    diag,
    lad_send,
    back_send,
    wts,
    onehot,
    e_bar,
    g_bar,
    wrow,
    pocc,
    rocc,
    cmap,
    held,
    turned,
    load_sem,
    w_sem,
    own_sem,
    a2a_send,
    a2a_recv,
    gat_send,
    gat_recv,
    lad_ssem,
    lad_rsem,
    back_ssem,
    back_rsem,
    held_rsem,
    pass_ssem,
    pass_own,
):
    c = lax.axis_index("chan")
    t = lax.axis_index("tile")
    core = lax.rem(c, 2)
    group = 512 // n_chan

    def target(move):
        x, y, k = move
        return lax.rem(c // 8 + y, 4) * 8 + lax.rem(c // 2 + x, 4) * 2 + lax.rem(core + k, 2)

    load_e = pltpu.make_async_copy(e_hbm, e_m, load_sem.at[0])
    load_g = pltpu.make_async_copy(g_hbm, g_m, load_sem.at[1])
    load_e.start()
    load_g.start()
    small = [
        pltpu.make_async_copy(src, dst, load_sem.at[n])
        for n, (src, dst) in enumerate(((pocc_hbm, pocc), (cmap_hbm, cmap), (rocc_hbm, rocc)), 2)
    ]
    for load in small:
        load.start()
    load_w = pltpu.make_async_copy(w_hbm, wts, w_sem)

    barrier = pltpu.get_barrier_semaphore()

    @pl.loop(1, n_chan)
    def _(k):
        pl.semaphore_signal(barrier, inc=1, device_id=(c ^ k, t), device_id_type=MESH)

    @pl.loop(1, 8)
    def _(k):
        pl.semaphore_signal(barrier, inc=1, device_id=(c, lax.rem(t + k, 8)), device_id_type=MESH)

    cols = lax.broadcasted_iota(jnp.int32, (1, 1024), 1)
    rows = lax.broadcasted_iota(jnp.int32, (BLK, 1), 0) + t * BLK
    load_e.wait()
    load_g.wait()
    small[0].wait()
    for h in range(4):
        size = sizes[h]
        col_live = (cols < size).astype(F32)
        row_live = (rows < size).astype(F32)
        wrow[h] = (1 - pocc[0, pl.ds(h, 1), :] - pocc[1, pl.ds(h, 1), :]).astype(F32) * col_live
        live = (row_live * col_live).astype(BF)
        e_m[h] = e_m[h] * live
        g_m[h] = g_m[h] * live

    load_w.start()
    pl.semaphore_wait(barrier, n_chan + 6)

    def gather(src, dst, which, phase):
        for h in (2 * phase, 2 * phase + 1):
            owner = 4 * (h % 2) + phase + 2 * core
            delta = lax.rem(t - owner + 8, 8)
            far = jnp.minimum(delta, 8 - delta)

            def send(j, h=h, owner=owner, delta=delta):
                pltpu.make_async_remote_copy(
                    src_ref=src.at[h, :, at128(lax.rem(owner + j, 8))],
                    dst_ref=dst.at[at128(delta), at128(j)],
                    send_sem=gat_send,
                    recv_sem=gat_recv.at[which],
                    device_id=(c, owner),
                    device_id_type=MESH,
                ).start()

            @pl.when(delta != 0)
            def _(send=send, far=far, delta=delta):
                send(delta)

                @pl.when(delta > 4 if which else delta < 4)
                def _():
                    send(8 - delta)

                @pl.loop(far + 1, 8 - far)
                def _(j):
                    send(j)

    gather(e_m, e_full, 0, 0)
    gather(g_m, g_full, 1, 0)
    gather(e_m, e_full, 0, 1)
    gather(g_m, g_full, 1, 1)

    own_place = pl.ds(pl.multiple_of(c * group, group), group)

    @pl.loop(0, 2)
    def _(q):
        side = pl.ds(pl.multiple_of(q * 512, 512), 512)
        for move in moves():
            s = target(move)
            first = pl.multiple_of(lax.rem(s * group, BLK), group)
            for n, (src, dst) in enumerate(((e_m, rec_e), (g_m, rec_g))):
                pltpu.make_async_remote_copy(
                    src_ref=src.at[(s * group) // BLK, pl.ds(first, group), side],
                    dst_ref=dst.at[own_place, side],
                    send_sem=a2a_send,
                    recv_sem=a2a_recv.at[q, n],
                    device_id=(s, t),
                    device_id_type=MESH,
                ).start()


    own_h = (c * group) // BLK
    own_rows = pl.ds(pl.multiple_of(lax.rem(c * group, BLK), group), group)
    rec_e[own_place, :] = e_m[own_h, own_rows, :]
    rec_g[own_place, :] = g_m[own_h, own_rows, :]

    small[1].wait()
    small[2].wait()
    for q in range(2):
        spots = lax.broadcasted_iota(jnp.int32, (512, 512), 0)
        onehot[q] = (spots == cmap[pl.ds(q, 1), :]).astype(F32).astype(BF)

    for h in range(4):
        weight = wrow[h].astype(BF)
        mine = dot_rows(e_m[h] * weight, g_m[h]) + dot_rows(g_m[h] * weight, e_m[h])
        diag[h] = mine.astype(BF)
        pltpu.make_async_copy(diag.at[h], lad_out.at[h, :, at128(t)], own_sem.at[2]).start()

    is_owner = lax.rem(t // 2, 2) == core
    own = 2 * lax.rem(t, 2) + t // 4

    def arrive(full, which):
        landed = full.at[pl.ds(0, 28 * 16), :]
        pltpu.make_async_copy(landed, landed, gat_recv.at[which]).wait()
        for a, b in pairs_of(which):
            block = full[pl.ds(a * BLK, BLK), pl.ds(b * BLK, BLK)].T
            full[pl.ds(b * BLK, BLK), pl.ds(a * BLK, BLK)] = block if which else -block

    @pl.when(is_owner)
    def _():
        for j in range(8):
            place = at128(lax.rem(t + j, 8))
            here = pl.ds(j * BLK, BLK)
            e_full[pl.ds(0, BLK), here] = e_m[own, :, place]
            g_full[pl.ds(0, BLK), here] = g_m[own, :, place]
        arrive(e_full, 0)
        for j in range(8):
            here = pl.ds(j * BLK, BLK)
            weight = wrow[own, :, at128(lax.rem(t + j, 8))].astype(BF)
            e_full[:, here] = e_full[:, here] * weight

    def cross(q):
        side = pl.ds(q * 512, 512)
        for n, rec in enumerate((rec_e, rec_g)):
            landed = rec.at[pl.ds(0, 512 - group), side]
            pltpu.make_async_copy(landed, landed, a2a_recv.at[q, n]).wait()
        turn = onehot[q]
        scale = wts[q]
        e_bar[...] = (jnp.dot(rec_e[:, side], turn, preferred_element_type=F32) * scale).astype(BF)
        g_bar[...] = (jnp.dot(rec_g[:, side], turn, preferred_element_type=F32) * scale).astype(BF)
        signs = (rocc[0, pl.ds(q, 1), :] - rocc[1, pl.ds(q, 1), :]).astype(F32).astype(BF)
        crossed = jnp.dot(e_bar[...] * signs, g_bar[...], preferred_element_type=F32)
        crossed = crossed - jnp.dot(g_bar[...] * signs, e_bar[...], preferred_element_type=F32)
        scaled = (crossed * scale).astype(BF)
        back_send[:, side] = dot_rows(scaled, turn).astype(BF)
        for move in moves():
            s = target(move)
            pltpu.make_async_remote_copy(
                src_ref=back_send.at[pl.ds(pl.multiple_of(s * group, group), group), side],
                dst_ref=back_out.at[own_place, side],
                send_sem=back_ssem,
                recv_sem=back_rsem,
                device_id=(s, t),
                device_id_type=MESH,
            ).start()

    def ladder():
        h = own
        arrive(g_full, 1)

        @pl.loop(0, 4)
        def _(step):
            jj = lax.rem(6 - step, 4)
            half = pl.ds(pl.multiple_of(jj * 256, 256), 256)
            total = jnp.dot(e_full[...], g_full[:, half], preferred_element_type=F32)
            total = total + dot_rows(g_full[...], e_full[half, :])
            lad_send[:, half] = total.astype(BF)

            def give(i, j, dst, sem):
                pltpu.make_async_remote_copy(
                    src_ref=lad_send.at[pl.ds(i * BLK, BLK), at128(j)],
                    dst_ref=dst,
                    send_sem=lad_ssem,
                    recv_sem=sem,
                    device_id=(c, lax.rem(t + i, 8)),
                    device_id_type=MESH,
                ).start()

            for i in (1, 7, 2, 6, 3, 5):
                for m in range(2):
                    j = 2 * jj + m
                    for n, k in enumerate(passed(i)):

                        @pl.when(j == k)
                        def _(i=i, j=j, n=n):
                            give(i, j, held.at[h, n], held_rsem.at[h])

            for i in (3, 5, 2, 6, 1, 7, 4):
                for m in range(2):
                    j = 2 * jj + m
                    plain = j == 0
                    if i != 4:
                        plain = j != i
                        for k in passed(i) + ((1, 2) if i == 3 else (6, 7) if i == 5 else ()):
                            plain = jnp.logical_and(plain, j != k)

                    @pl.when(plain)
                    def _(i=i, j=j):
                        give(i, j, lad_out.at[h, :, at128(lax.rem(t + j, 8))], lad_rsem.at[h])

            for m in range(2):
                j = 2 * jj + m

                @pl.when(j != 0)
                def _(j=j):
                    pltpu.make_async_copy(
                        lad_send.at[pl.ds(0, BLK), at128(j)],
                        lad_out.at[h, :, at128(lax.rem(t + j, 8))],
                        own_sem.at[0],
                    ).start()

    def pass_on(h):
        owner = 4 * (h % 2) + h // 2 + 2 * core
        delta = lax.rem(t - owner + 8, 8)
        far = jnp.minimum(delta, 8 - delta)
        beyond = jnp.where(delta < 4, 3, 5)

        def pass_block(n, place, h=h):
            turned[h, n] = held[h, n].T
            pltpu.make_async_copy(held.at[h, n], lad_out.at[h, :, at128(place)], pass_own).start()
            pltpu.make_async_remote_copy(
                src_ref=turned.at[h, n],
                dst_ref=lad_out.at[h, :, at128(t)],
                send_sem=pass_ssem,
                recv_sem=lad_rsem.at[h],
                device_id=(c, place),
                device_id_type=MESH,
            ).start()

        @pl.when(far == 3)
        def _(h=h, owner=owner, pass_block=pass_block):
            pltpu.make_async_copy(held.at[h, 0], held.at[h, 0], held_rsem.at[h]).wait()
            pass_block(0, lax.rem(owner + 4, 8))

        @pl.when(jnp.logical_or(far == 1, far == 2))
        def _(h=h, owner=owner, beyond=beyond, pass_block=pass_block):
            pltpu.make_async_copy(held.at[h], held.at[h], held_rsem.at[h]).wait()
            pass_block(0, lax.rem(owner + 4, 8))
            pass_block(1, lax.rem(owner + beyond, 8))

    late = lax.rem(t, 2) == 1

    @pl.when(jnp.logical_and(is_owner, jnp.logical_not(late)))
    def _():
        ladder()

    load_w.wait()
    cross(0)

    @pl.when(jnp.logical_and(is_owner, late))
    def _():
        ladder()

    pass_on(0)
    pass_on(1)
    cross(1)
    pass_on(2)
    pass_on(3)

    keep = pltpu.make_async_copy(back_send.at[own_place, :], back_out.at[own_place, :], own_sem.at[1])
    keep.start()

    def drain(ref, count, sem):
        piece = ref.at[pl.ds(0, count), :]
        pltpu.make_async_copy(piece, piece, sem).wait()

    @pl.when(is_owner)
    def _():
        drain(lad_send, 3 * 16, pass_own)
        drain(lad_send, 7 * 16, own_sem.at[0])

    @pl.when(jnp.logical_not(is_owner))
    def _():
        drain(lad_send, 7 * 16, pass_own)

    keep.wait()
    drain(lad_send, 4 * 16, own_sem.at[2])
    drain(rec_e, 512 - group, back_rsem)

    for h in range(4):
        delta = lax.rem(t - (4 * (h % 2) + h // 2 + 2 * core) + 8, 8)
        far = jnp.minimum(delta, 8 - delta)

        @pl.when(jnp.logical_or(far == 1, far == 2))
        def _(h=h):
            drain(lad_send, 5 * 16, lad_rsem.at[h])

        @pl.when(far == 3)
        def _(h=h):
            drain(lad_send, 6 * 16, lad_rsem.at[h])

        @pl.when(far == 4)
        def _(h=h):
            drain(lad_send, 7 * 16, lad_rsem.at[h])

        size = sizes[h]
        live = (rows < size).astype(F32) * (cols < size).astype(F32)
        total = lad_out[h].astype(F32) + back_out[pl.ds(h * BLK, BLK), :].astype(F32)
        out[h] = jnp.where(live > 0, total, 0.0).astype(BF)

    for n in range(2):
        drain(rec_e, 512 - group, a2a_send)

    @pl.when(is_owner)
    def _():
        drain(lad_send, 20 * 16, gat_send)
        drain(lad_send, 39 * 16, lad_ssem)
        drain(lad_send, 3 * 16, pass_ssem)

    @pl.when(jnp.logical_not(is_owner))
    def _():
        drain(lad_send, 36 * 16, gat_send)
        drain(lad_send, 7 * 16, pass_ssem)

    drain(rec_e, 512 - group, back_ssem)


def exchange(n_chan, *args):
    far = pl.BlockSpec(memory_space=pltpu.HBM)
    smem = pl.BlockSpec(memory_space=pltpu.SMEM)
    dma = pltpu.SemaphoreType.DMA
    return pl.pallas_call(
        functools.partial(kernel, n_chan),
        name="commutator_exchange",
        out_shape=jax.ShapeDtypeStruct((4, BLK, 1024), BF),
        in_specs=[far, far, smem, far, far, far, far],
        out_specs=pl.BlockSpec(memory_space=pltpu.VMEM),
        scratch_shapes=[
            pltpu.VMEM((4, BLK, 1024), BF),
            pltpu.VMEM((512, 1024), BF),
            pltpu.VMEM((4, BLK, 1024), BF),
            pltpu.VMEM((4, BLK, 1024), BF),
            pltpu.VMEM((512, 1024), BF),
            pltpu.VMEM((512, 1024), BF),
            pltpu.VMEM((1024, 1024), BF),
            pltpu.VMEM((1024, 1024), BF),
            pltpu.VMEM((4, BLK, BLK), BF),
            pltpu.VMEM((1024, 1024), BF),
            pltpu.VMEM((512, 1024), BF),
            pltpu.VMEM((2, 512, 512), F32),
            pltpu.VMEM((2, 512, 512), BF),
            pltpu.VMEM((512, 512), BF),
            pltpu.VMEM((512, 512), BF),
            pltpu.VMEM((4, 1, 1024), F32),
            pltpu.VMEM((2, 4, 1024), jnp.int32),
            pltpu.VMEM((2, 2, 512), jnp.int32),
            pltpu.VMEM((2, 512), jnp.int32),
            pltpu.VMEM((4, 2, BLK, BLK), BF),
            pltpu.VMEM((4, 2, BLK, BLK), BF),
            dma((5,)),
            dma,
            dma((3,)),
            dma,
            dma((2, 2)),
            dma,
            dma((2,)),
            dma,
            dma((4,)),
            dma,
            dma,
            dma((4,)),
            dma,
            dma,
        ],
        compiler_params=pltpu.CompilerParams(
            collective_id=0, has_side_effects=True, vmem_limit_bytes=VMEM_BYTES
        ),
    )(*[pltpu.with_memory_space_constraint(a, pltpu.HBM) for a in args])


def per_device(
    n_chan,
    generator,
    hamiltonian,
    chan_sizes,
    pair_occupation,
    recoupled_occupation,
    recouple_map,
    recouple_weights,
):
    return exchange(
        n_chan,
        generator,
        hamiltonian,
        chan_sizes,
        pair_occupation,
        recoupled_occupation,
        recouple_map,
        recouple_weights,
    )


def solution(mesh):
    return jax.shard_map(
        functools.partial(per_device, mesh.shape["chan"]),
        mesh=mesh,
        in_specs=(
            P("chan", "tile", None),
            P("chan", "tile", None),
            P("chan"),
            P(None, "chan", None),
            P(None, ("chan", "tile"), None),
            P(("chan", "tile"), None),
            P(("chan", "tile"), None, None),
        ),
        out_specs=P("chan", "tile", None),
        check_vma=False,
    )
```

```python
import functools

import jax
import jax.numpy as jnp
from jax import lax
from jax.experimental import pallas as pl
from jax.experimental.pallas import tpu as pltpu
from jax.sharding import PartitionSpec as P

MESH = pl.DeviceIdType.MESH
BF = jnp.bfloat16
F32 = jnp.float32
BLK = 128
VMEM_BYTES = 30 * 1024 * 1024

ORDER = (0, 1, 7, 2, 6, 3, 5, 4)


def pairs_of(flip_ties):
    found = []
    for i in range(8):
        for j in range(i + 1, 8):
            a, b = ORDER[i], ORDER[j]
            if flip_ties and a + b == 8:
                a, b = b, a
            found.append((a, b))
    return found


def hops(move):
    return min(move[0], 4 - move[0]) + min(move[1], 4 - move[1])


def moves():
    listed = []
    everything = [(x, y, k) for y in range(4) for x in range(4) for k in range(2) if (x, y, k) != (0, 0, 0)]
    for far in (1, 2, 3, 4, 0):
        left = [m for m in everything if hops(m) == far]
        taken = []
        while left:
            recent = taken[-3:][::-1]
            cost = lambda m: sum(((m[0] == p[0]) + (m[1] == p[1])) * (3 - i) for i, p in enumerate(recent))
            taken.append(min(left, key=cost))
            left.remove(taken[-1])
        listed += taken
    return listed[::-1]


def passed(i):
    return {0: (), 4: (), 3: (4,), 5: (4,)}.get(i, (4, 3 if i < 4 else 5))


def dot_rows(a, b):
    return lax.dot_general(a, b, (((1,), (1,)), ((), ())), preferred_element_type=F32)


def at128(index):
    return pl.ds(pl.multiple_of(index * BLK, BLK), BLK)


def kernel(
    n_chan,
    e_hbm,
    g_hbm,
    sizes,
    pocc_hbm,
    rocc_hbm,
    cmap_hbm,
    w_hbm,
    out,
    lad_out,
    back_out,
    e_m,
    g_m,
    rec_e,
    rec_g,
    e_full,
    g_full,
    diag,
    lad_send,
    back_send,
    wts,
    onehot,
    e_bar,
    g_bar,
    wrow,
    pocc,
    rocc,
    cmap,
    held,
    turned,
    load_sem,
    w_sem,
    own_sem,
    a2a_send,
    a2a_recv,
    gat_send,
    gat_recv,
    lad_ssem,
    lad_rsem,
    back_ssem,
    back_rsem,
    held_rsem,
    pass_ssem,
    pass_own,
):
    c = lax.axis_index("chan")
    t = lax.axis_index("tile")
    core = lax.rem(c, 2)
    group = 512 // n_chan

    def target(move):
        x, y, k = move
        return lax.rem(c // 8 + y, 4) * 8 + lax.rem(c // 2 + x, 4) * 2 + lax.rem(core + k, 2)

    load_e = pltpu.make_async_copy(e_hbm, e_m, load_sem.at[0])
    load_g = pltpu.make_async_copy(g_hbm, g_m, load_sem.at[1])
    load_e.start()
    load_g.start()
    small = [
        pltpu.make_async_copy(src, dst, load_sem.at[n])
        for n, (src, dst) in enumerate(((pocc_hbm, pocc), (cmap_hbm, cmap), (rocc_hbm, rocc)), 2)
    ]
    for load in small:
        load.start()
    load_w = pltpu.make_async_copy(w_hbm, wts, w_sem)

    barrier = pltpu.get_barrier_semaphore()

    @pl.loop(1, n_chan)
    def _(k):
        pl.semaphore_signal(barrier, inc=1, device_id=(c ^ k, t), device_id_type=MESH)

    @pl.loop(1, 8)
    def _(k):
        pl.semaphore_signal(barrier, inc=1, device_id=(c, lax.rem(t + k, 8)), device_id_type=MESH)

    cols = lax.broadcasted_iota(jnp.int32, (1, 1024), 1)
    rows = lax.broadcasted_iota(jnp.int32, (BLK, 1), 0) + t * BLK
    load_e.wait()
    load_g.wait()
    small[0].wait()
    for h in range(4):
        size = sizes[h]
        col_live = (cols < size).astype(F32)
        row_live = (rows < size).astype(F32)
        wrow[h] = (1 - pocc[0, pl.ds(h, 1), :] - pocc[1, pl.ds(h, 1), :]).astype(F32) * col_live
        live = (row_live * col_live).astype(BF)
        e_m[h] = e_m[h] * live
        g_m[h] = g_m[h] * live

    load_w.start()
    pl.semaphore_wait(barrier, n_chan + 6)

    def gather(src, dst, which, phase):
        for h in (2 * phase, 2 * phase + 1):
            owner = 4 * (h % 2) + phase + 2 * core
            delta = lax.rem(t - owner + 8, 8)
            far = jnp.minimum(delta, 8 - delta)

            def send(j, h=h, owner=owner, delta=delta):
                pltpu.make_async_remote_copy(
                    src_ref=src.at[h, :, at128(lax.rem(owner + j, 8))],
                    dst_ref=dst.at[at128(delta), at128(j)],
                    send_sem=gat_send,
                    recv_sem=gat_recv.at[which],
                    device_id=(c, owner),
                    device_id_type=MESH,
                ).start()

            @pl.when(delta != 0)
            def _(send=send, far=far, delta=delta):
                send(delta)

                @pl.when(delta > 4 if which else delta < 4)
                def _():
                    send(8 - delta)

                @pl.loop(far + 1, 8 - far)
                def _(j):
                    send(j)

    gather(e_m, e_full, 0, 0)
    gather(g_m, g_full, 1, 0)
    gather(e_m, e_full, 0, 1)
    gather(g_m, g_full, 1, 1)

    own_place = pl.ds(pl.multiple_of(c * group, group), group)

    @pl.loop(0, 2)
    def _(q):
        side = pl.ds(pl.multiple_of(q * 512, 512), 512)
        for move in moves():
            s = target(move)
            first = pl.multiple_of(lax.rem(s * group, BLK), group)
            for n, (src, dst) in enumerate(((e_m, rec_e), (g_m, rec_g))):
                pltpu.make_async_remote_copy(
                    src_ref=src.at[(s * group) // BLK, pl.ds(first, group), side],
                    dst_ref=dst.at[own_place, side],
                    send_sem=a2a_send,
                    recv_sem=a2a_recv.at[q, n],
                    device_id=(s, t),
                    device_id_type=MESH,
                ).start()


    own_h = (c * group) // BLK
    own_rows = pl.ds(pl.multiple_of(lax.rem(c * group, BLK), group), group)
    rec_e[own_place, :] = e_m[own_h, own_rows, :]
    rec_g[own_place, :] = g_m[own_h, own_rows, :]

    small[1].wait()
    small[2].wait()
    for q in range(2):
        spots = lax.broadcasted_iota(jnp.int32, (512, 512), 0)
        onehot[q] = (spots == cmap[pl.ds(q, 1), :]).astype(F32).astype(BF)

    for h in range(4):
        weight = wrow[h].astype(BF)
        mine = dot_rows(e_m[h] * weight, g_m[h]) + dot_rows(g_m[h] * weight, e_m[h])
        diag[h] = mine.astype(BF)
        pltpu.make_async_copy(diag.at[h], lad_out.at[h, :, at128(t)], own_sem.at[2]).start()

    is_owner = lax.rem(t // 2, 2) == core
    own = 2 * lax.rem(t, 2) + t // 4

    def arrive(full, which):
        landed = full.at[pl.ds(0, 28 * 16), :]
        pltpu.make_async_copy(landed, landed, gat_recv.at[which]).wait()
        for a, b in pairs_of(which):
            block = full[pl.ds(a * BLK, BLK), pl.ds(b * BLK, BLK)].T
            full[pl.ds(b * BLK, BLK), pl.ds(a * BLK, BLK)] = block if which else -block

    @pl.when(is_owner)
    def _():
        for j in range(8):
            place = at128(lax.rem(t + j, 8))
            here = pl.ds(j * BLK, BLK)
            e_full[pl.ds(0, BLK), here] = e_m[own, :, place]
            g_full[pl.ds(0, BLK), here] = g_m[own, :, place]
        arrive(e_full, 0)
        for j in range(8):
            here = pl.ds(j * BLK, BLK)
            weight = wrow[own, :, at128(lax.rem(t + j, 8))].astype(BF)
            e_full[:, here] = e_full[:, here] * weight

    def cross(q):
        side = pl.ds(q * 512, 512)
        for n, rec in enumerate((rec_e, rec_g)):
            landed = rec.at[pl.ds(0, 512 - group), side]
            pltpu.make_async_copy(landed, landed, a2a_recv.at[q, n]).wait()
        turn = onehot[q]
        scale = wts[q]
        e_bar[...] = (jnp.dot(rec_e[:, side], turn, preferred_element_type=F32) * scale).astype(BF)
        g_bar[...] = (jnp.dot(rec_g[:, side], turn, preferred_element_type=F32) * scale).astype(BF)
        signs = (rocc[0, pl.ds(q, 1), :] - rocc[1, pl.ds(q, 1), :]).astype(F32).astype(BF)
        crossed = jnp.dot(e_bar[...] * signs, g_bar[...], preferred_element_type=F32)
        crossed = crossed - jnp.dot(g_bar[...] * signs, e_bar[...], preferred_element_type=F32)
        scaled = (crossed * scale).astype(BF)
        back_send[:, side] = dot_rows(scaled, turn).astype(BF)
        for move in moves():
            s = target(move)
            pltpu.make_async_remote_copy(
                src_ref=back_send.at[pl.ds(pl.multiple_of(s * group, group), group), side],
                dst_ref=back_out.at[own_place, side],
                send_sem=back_ssem,
                recv_sem=back_rsem,
                device_id=(s, t),
                device_id_type=MESH,
            ).start()

    def ladder():
        h = own
        arrive(g_full, 1)

        for jj in (2, 1, 0, 3):
            half = pl.ds(jj * 256, 256)
            total = jnp.dot(e_full[...], g_full[:, half], preferred_element_type=F32)
            total = total + dot_rows(g_full[...], e_full[half, :])
            lad_send[:, half] = total.astype(BF)

            def give(i, j, dst, sem):
                pltpu.make_async_remote_copy(
                    src_ref=lad_send.at[pl.ds(i * BLK, BLK), at128(j)],
                    dst_ref=dst,
                    send_sem=lad_ssem,
                    recv_sem=sem,
                    device_id=(c, lax.rem(t + i, 8)),
                    device_id_type=MESH,
                ).start()

            for i in (1, 7, 2, 6, 3, 5):
                for m in range(2):
                    j = 2 * jj + m
                    for n, k in enumerate(passed(i)):
                        if j == k:
                            give(i, j, held.at[h, n], held_rsem.at[h])

            for i in (3, 5, 2, 6, 1, 7, 4):
                for m in range(2):
                    j = 2 * jj + m
                    plain = j == 0
                    if i != 4:
                        plain = j != i
                        for k in passed(i) + ((1, 2) if i == 3 else (6, 7) if i == 5 else ()):
                            plain = plain and j != k

                    if plain:
                        give(i, j, lad_out.at[h, :, at128(lax.rem(t + j, 8))], lad_rsem.at[h])

            for m in range(2):
                j = 2 * jj + m
                if j != 0:
                    pltpu.make_async_copy(
                        lad_send.at[pl.ds(0, BLK), at128(j)],
                        lad_out.at[h, :, at128(lax.rem(t + j, 8))],
                        own_sem.at[0],
                    ).start()

    def pass_on(h):
        owner = 4 * (h % 2) + h // 2 + 2 * core
        delta = lax.rem(t - owner + 8, 8)
        far = jnp.minimum(delta, 8 - delta)
        beyond = jnp.where(delta < 4, 3, 5)

        def pass_block(n, place, h=h):
            turned[h, n] = held[h, n].T
            pltpu.make_async_copy(held.at[h, n], lad_out.at[h, :, at128(place)], pass_own).start()
            pltpu.make_async_remote_copy(
                src_ref=turned.at[h, n],
                dst_ref=lad_out.at[h, :, at128(t)],
                send_sem=pass_ssem,
                recv_sem=lad_rsem.at[h],
                device_id=(c, place),
                device_id_type=MESH,
            ).start()

        @pl.when(far == 3)
        def _(h=h, owner=owner, pass_block=pass_block):
            pltpu.make_async_copy(held.at[h, 0], held.at[h, 0], held_rsem.at[h]).wait()
            pass_block(0, lax.rem(owner + 4, 8))

        @pl.when(jnp.logical_or(far == 1, far == 2))
        def _(h=h, owner=owner, beyond=beyond, pass_block=pass_block):
            pltpu.make_async_copy(held.at[h], held.at[h], held_rsem.at[h]).wait()
            pass_block(0, lax.rem(owner + 4, 8))
            pass_block(1, lax.rem(owner + beyond, 8))

    late = lax.rem(t, 2) == 1

    @pl.when(jnp.logical_and(is_owner, jnp.logical_not(late)))
    def _():
        ladder()

    load_w.wait()
    cross(0)

    @pl.when(jnp.logical_and(is_owner, late))
    def _():
        ladder()

    pass_on(0)
    pass_on(1)
    cross(1)
    pass_on(2)
    pass_on(3)

    keep = pltpu.make_async_copy(back_send.at[own_place, :], back_out.at[own_place, :], own_sem.at[1])
    keep.start()

    def drain(ref, count, sem):
        piece = ref.at[pl.ds(0, count), :]
        pltpu.make_async_copy(piece, piece, sem).wait()

    for n in range(2):
        drain(rec_e, 512 - group, a2a_send)

    @pl.when(is_owner)
    def _():
        drain(lad_send, 20 * 16, gat_send)
        drain(lad_send, 39 * 16, lad_ssem)
        drain(lad_send, 3 * 16, pass_ssem)
        drain(lad_send, 3 * 16, pass_own)
        drain(lad_send, 7 * 16, own_sem.at[0])

    @pl.when(jnp.logical_not(is_owner))
    def _():
        drain(lad_send, 36 * 16, gat_send)
        drain(lad_send, 7 * 16, pass_ssem)
        drain(lad_send, 7 * 16, pass_own)

    keep.wait()
    drain(lad_send, 4 * 16, own_sem.at[2])
    drain(rec_e, 512 - group, back_ssem)
    drain(rec_e, 512 - group, back_rsem)

    for h in range(4):
        delta = lax.rem(t - (4 * (h % 2) + h // 2 + 2 * core) + 8, 8)
        far = jnp.minimum(delta, 8 - delta)

        @pl.when(jnp.logical_or(far == 1, far == 2))
        def _(h=h):
            drain(lad_send, 5 * 16, lad_rsem.at[h])

        @pl.when(far == 3)
        def _(h=h):
            drain(lad_send, 6 * 16, lad_rsem.at[h])

        @pl.when(far == 4)
        def _(h=h):
            drain(lad_send, 7 * 16, lad_rsem.at[h])

        size = sizes[h]
        live = (rows < size).astype(F32) * (cols < size).astype(F32)
        total = lad_out[h].astype(F32) + back_out[pl.ds(h * BLK, BLK), :].astype(F32)
        out[h] = jnp.where(live > 0, total, 0.0).astype(BF)


def exchange(n_chan, *args):
    far = pl.BlockSpec(memory_space=pltpu.HBM)
    smem = pl.BlockSpec(memory_space=pltpu.SMEM)
    dma = pltpu.SemaphoreType.DMA
    return pl.pallas_call(
        functools.partial(kernel, n_chan),
        name="commutator_exchange",
        out_shape=jax.ShapeDtypeStruct((4, BLK, 1024), BF),
        in_specs=[far, far, smem, far, far, far, far],
        out_specs=pl.BlockSpec(memory_space=pltpu.VMEM),
        scratch_shapes=[
            pltpu.VMEM((4, BLK, 1024), BF),
            pltpu.VMEM((512, 1024), BF),
            pltpu.VMEM((4, BLK, 1024), BF),
            pltpu.VMEM((4, BLK, 1024), BF),
            pltpu.VMEM((512, 1024), BF),
            pltpu.VMEM((512, 1024), BF),
            pltpu.VMEM((1024, 1024), BF),
            pltpu.VMEM((1024, 1024), BF),
            pltpu.VMEM((4, BLK, BLK), BF),
            pltpu.VMEM((1024, 1024), BF),
            pltpu.VMEM((512, 1024), BF),
            pltpu.VMEM((2, 512, 512), F32),
            pltpu.VMEM((2, 512, 512), BF),
            pltpu.VMEM((512, 512), BF),
            pltpu.VMEM((512, 512), BF),
            pltpu.VMEM((4, 1, 1024), F32),
            pltpu.VMEM((2, 4, 1024), jnp.int32),
            pltpu.VMEM((2, 2, 512), jnp.int32),
            pltpu.VMEM((2, 512), jnp.int32),
            pltpu.VMEM((4, 2, BLK, BLK), BF),
            pltpu.VMEM((4, 2, BLK, BLK), BF),
            dma((5,)),
            dma,
            dma((3,)),
            dma,
            dma((2, 2)),
            dma,
            dma((2,)),
            dma,
            dma((4,)),
            dma,
            dma,
            dma((4,)),
            dma,
            dma,
        ],
        compiler_params=pltpu.CompilerParams(
            collective_id=0, has_side_effects=True, vmem_limit_bytes=VMEM_BYTES
        ),
    )(*[pltpu.with_memory_space_constraint(a, pltpu.HBM) for a in args])


def per_device(
    n_chan,
    generator,
    hamiltonian,
    chan_sizes,
    pair_occupation,
    recoupled_occupation,
    recouple_map,
    recouple_weights,
):
    return exchange(
        n_chan,
        generator,
        hamiltonian,
        chan_sizes,
        pair_occupation,
        recoupled_occupation,
        recouple_map,
        recouple_weights,
    )


def solution(mesh):
    return jax.shard_map(
        functools.partial(per_device, mesh.shape["chan"]),
        mesh=mesh,
        in_specs=(
            P("chan", "tile", None),
            P("chan", "tile", None),
            P("chan"),
            P(None, "chan", None),
            P(None, ("chan", "tile"), None),
            P(("chan", "tile"), None),
            P(("chan", "tile"), None, None),
        ),
        out_specs=P("chan", "tile", None),
        check_vma=False,
    )
```
